128 devices in a mesh: lat: 16 (over x, z), lon: 8 (over y, core).
Axes of the slice: x: 4, y: 4, z: 4, core: 2. Of those that a mesh axis runs over, the one named last changes fastest.
Arguments:
- grid_fields: float32 [8, 32, 6144], P(None, 'lat', 'lon'), may hold values from -6 to 6
- sun_cosine: float32 [32, 6144], P('lat', 'lon'), may hold values from 0.1 to 1
- surface_albedo: float32 [32, 6144], P('lat', 'lon'), may hold values from 0.05 to 0.8
- gas_absorb: float32 [112], replicated, may hold values from 0.02 to 4
- solar_weight: float32 [112], replicated, may hold values from 0.1 to 1
- helper_map: int32 [32, 48], P('lat', 'lon'), may hold values from -1 to 127, as said below
- row_lat: int32 [32], replicated, may hold values from 1008 to 1551, as said below
- wave_owner: int32 [1280], replicated, may hold values from 0 to 15, as said below
Outputs:
- spectral: float32 [1920, 8, 2, 1280], P(('lat', 'lon'))
The draws below stay inside these ranges and needn't reach their ends.
Inputs may be any that keep to these rules, and one draw needn't show every extreme that they name: `helper_map`: the lit blocks are the same 48 / 2 cyclically consecutive block columns in every row. Lit blocks are numbered in the order of devices along lat+lon and within a device by row, then block, and the k-th goes to helper k mod 128: a device sends at most 1 lit blocks to one helper (a device whose blocks are all lit does so), and every helper receives exactly 6 lit blocks. `row_lat`: increasing and distinct, 32 of the 544 latitudes nearest the equator, always holding the first and last of them and latitude 2560 / 2 - 1. `wave_owner`: half of the owners hold exactly 120 wavenumbers and the other half exactly 40; which wavenumbers is arbitrary.
All inputs are finite; a program needn't handle non-finite values.
Results may differ from the reference program's by a relative error of at most 0.0006.
Values sent between devices are 32-bit elements; how exact they have to be, the bound alone decides.
No kernel may reach another device: no remote copies, remote signals or barrier semaphores. Data moves between devices by JAX's collectives and lax.ppermute only.
A program may use at most 64 MiB of HBM per device.

```python
import math
import jax
import jax.numpy as jnp
from jax import lax

LEV = 4
G = 112
BLOCK = 128
NLAT_FULL = 2560
NLON_PAD = 6144
MW = 1280
CAND = 544
ROWS_DEV = 2
K = 8
ROWS_T = 32
NA = 48
SB = 6
HELPERS = 128
MCAP = 120
N_LAT = 16
N_LON = 8


def draw_row_lat(key, part):
    first_lat = NLAT_FULL // 2 - CAND // 2
    centre = CAND // 2 - 1
    others = jnp.concatenate([jnp.arange(1, centre, dtype=jnp.int32), jnp.arange(centre + 1, CAND - 1, dtype=jnp.int32)])
    picked = jax.random.permutation(jax.random.fold_in(key, 11), others)[:ROWS_T - 3]
    forced = jnp.array([0, centre, CAND - 1], dtype=jnp.int32)
    chosen = jnp.sort(jnp.concatenate([forced, picked]))
    return (chosen + first_lat).astype(jnp.int32)


def draw_helper_map(key, part):
    start_col = jax.random.randint(jax.random.fold_in(key, 21), (), 0, NA)
    col_ids = jnp.arange(NA, dtype=jnp.int32)
    lit_col = ((col_ids - start_col) % NA < NA // 2).astype(jnp.int32)
    lit_grid = jnp.broadcast_to(lit_col[None, :], (ROWS_T, NA))
    ordered = lit_grid.reshape(N_LAT, ROWS_DEV, N_LON, SB).transpose(0, 2, 1, 3).reshape(-1)
    lit_rank = jnp.cumsum(ordered) - 1
    assigned = jnp.where(ordered > 0, lit_rank % HELPERS, -1)
    return assigned.reshape(N_LAT, N_LON, ROWS_DEV, SB).transpose(0, 2, 1, 3).reshape(ROWS_T, NA).astype(jnp.int32)


def draw_wave_owner(key, part):
    big_flag = jax.random.permutation(jax.random.fold_in(key, 31), N_LAT) < N_LAT // 2
    owner_count = jnp.where(big_flag, 3 * MW // (2 * N_LAT), MW // (2 * N_LAT)).astype(jnp.int32)
    bounds = jnp.cumsum(owner_count)
    positions = jnp.arange(MW, dtype=jnp.int32)
    owner_at = jnp.sum((positions[:, None] >= bounds[None, :]).astype(jnp.int32), axis=1)
    shuffle = jax.random.permutation(jax.random.fold_in(key, 32), MW)
    return jnp.zeros((MW,), jnp.int32).at[shuffle].set(owner_at).astype(jnp.int32)


def shard_levels(key, extent, cuts, smallest, top_value):
    loudness, own = 1.0, jax.random.fold_in(key, 6)
    for dim, parts in cuts:
        steps = jnp.exp(jax.random.uniform(jax.random.fold_in(own, dim), (parts,), jnp.float32, smallest / len(cuts), top_value / len(cuts)))
        loudness = loudness * jnp.repeat(steps, extent[dim] // parts).reshape([-1 if axis == dim else 1 for axis in range(len(extent))])
    return loudness


def bell_draw(stream_key, dims, scale, limit, split=(), kind=jnp.bfloat16):
    loudness = shard_levels(stream_key, dims, split, -0.22, 0.18) if split else 1.0
    entries = jax.random.normal(stream_key, dims, jnp.float32) * scale * loudness
    return jnp.minimum(jnp.maximum(entries, -limit), limit).astype(kind)


def setup_inputs(seed: int = 0) -> dict:
    key_list = jax.random.split(jax.random.key(seed), 9)
    return {
        "grid_fields": bell_draw(key_list[0], (K, ROWS_T, NLON_PAD), 1.0, 6.0, ((1, 16), (2, 8)), jnp.float32),
        "sun_cosine": jnp.clip(0.1 + 0.9 * jax.random.uniform(key_list[1], (ROWS_T, NLON_PAD), jnp.float32) ** shard_levels(key_list[1], (ROWS_T, NLON_PAD), ((0, 16), (1, 8)), -0.2, 0.2), 0.1, 1.0),
        "surface_albedo": jnp.clip(0.05 + 0.75 * jax.random.uniform(key_list[2], (ROWS_T, NLON_PAD), jnp.float32) ** shard_levels(key_list[2], (ROWS_T, NLON_PAD), ((0, 16), (1, 8)), -0.2, 0.2), 0.05, 0.8),
        "gas_absorb": jnp.clip(jnp.exp(jax.random.uniform(key_list[3], (G,), jnp.float32, math.log(0.02), math.log(4.0))), 0.02, 4.0),
        "solar_weight": jnp.clip(jnp.exp(jax.random.uniform(key_list[4], (G,), jnp.float32, math.log(0.1), math.log(1.0))), 0.1, 1.0),
        "helper_map": draw_helper_map(jax.random.fold_in(key_list[8], 71), 0),
        "row_lat": draw_row_lat(jax.random.fold_in(key_list[8], 71), 0),
        "wave_owner": draw_wave_owner(jax.random.fold_in(key_list[8], 71), 0),
    }


diffusivity = 1.66
scatter_share = 0.2
heat_gain = 10.0
highest = lax.Precision.HIGHEST

def radiate(humidity, sun_cos, ground, gas_absorb, solar_weight):
    shares = solar_weight / jnp.sum(solar_weight)
    levels = humidity.shape[0]
    directs = [shares[:, None] * sun_cos[None, :]]
    down_flux = [jnp.zeros_like(directs[0])]
    trans_list = []
    sources = []
    for layer_idx in range(levels):
        optical = gas_absorb[:, None] * jax.nn.softplus(humidity[layer_idx])[None, :]
        trans_dir = jnp.exp(-optical / sun_cos[None, :])
        trans_dif = jnp.exp(-diffusivity * optical)
        source = scatter_share * directs[-1] * (1.0 - trans_dir)
        down_flux.append(down_flux[-1] * trans_dif + source)
        directs.append(directs[-1] * trans_dir)
        trans_list.append(trans_dif)
        sources.append(source)
    upward = [None] * (levels + 1)
    upward[levels] = ground[None, :] * (directs[levels] + down_flux[levels])
    for layer_idx in range(levels - 1, -1, -1):
        upward[layer_idx] = upward[layer_idx + 1] * trans_list[layer_idx] + sources[layer_idx]
    net_flux = [directs[level_idx] + down_flux[level_idx] - upward[level_idx] for level_idx in range(levels + 1)]
    heating = [heat_gain * lax.optimization_barrier(jnp.sum(net_flux[level_idx] - net_flux[level_idx + 1], axis=0)) for level_idx in range(levels)]
    return jnp.stack(heating)

def inner_table(count):
    wave_ids = jnp.arange(MW, dtype=jnp.int32)
    offsets = jnp.arange(BLOCK, dtype=jnp.int32)
    phase_int = offsets[:, None] * wave_ids[None, :] % count
    angles = phase_int.astype(jnp.float32) * (2.0 * math.pi) / count.astype(jnp.float32)
    return jnp.concatenate([jnp.cos(angles), -jnp.sin(angles)], axis=1)

def block_twiddle(count, block_ids):
    wave_ids = jnp.arange(MW, dtype=jnp.int32)
    phase_int = block_ids[:, None] * BLOCK * wave_ids[None, :] % count
    angles = phase_int.astype(jnp.float32) * (2.0 * math.pi) / count.astype(jnp.float32)
    return (jnp.cos(angles), jnp.sin(angles))

def row_transform(rows_x, counts, first_block):
    row_count, vector_count, col_count = rows_x.shape
    block_count = col_count // BLOCK
    group_size = math.gcd(row_count, 2)
    block_ids = first_block + jnp.arange(block_count, dtype=jnp.int32)
    col_ids = first_block * BLOCK + jnp.arange(col_count, dtype=jnp.int32)

    def one_group(pair_args):
        values, lengths = pair_args
        masked = jnp.where(col_ids[None, None, :] < lengths[:, None, None], values, 0.0)
        pieces = masked.reshape(group_size, vector_count, block_count, BLOCK)
        tables = jax.vmap(inner_table)(lengths)
        partial_y = jnp.einsum('gvab,gbm->gvam', pieces, tables, precision=highest)
        cos_t, sin_t = jax.vmap(lambda length: block_twiddle(length, block_ids))(lengths)
        real_y = partial_y[..., :MW]
        imag_y = partial_y[..., MW:]
        cos_b = cos_t[:, None]
        sin_b = sin_t[:, None]
        real_x = lax.optimization_barrier(jnp.sum(cos_b * real_y + sin_b * imag_y, axis=2))
        imag_x = lax.optimization_barrier(jnp.sum(cos_b * imag_y - sin_b * real_y, axis=2))
        return jnp.stack([real_x, imag_x], axis=2)
    transformed = lax.map(one_group, (rows_x.reshape(row_count // group_size, group_size, vector_count, col_count), counts.reshape(row_count // group_size, group_size)))
    return transformed.reshape(row_count, vector_count, 2, MW)

def legendre(inputs, wave_ids, cos_lat, sin_lat):
    slot_count, col_count, row_count = inputs.shape
    mfloat = wave_ids.astype(jnp.float32)
    log_start = 0.5 * (lax.lgamma(mfloat + 1.5) - lax.lgamma(jnp.ones_like(mfloat) * 1.5) - lax.lgamma(mfloat + 1.0) + jnp.log(2.0 - (wave_ids == 0).astype(jnp.float32)))
    start_vals = jnp.exp(log_start[:, None] + mfloat[:, None] * jnp.log(sin_lat)[None, :])
    unroll = math.gcd(MW, 64)
    turn_count = MW // unroll

    def advance(previous, current, step_idx):
        degree = mfloat + (step_idx + 1).astype(jnp.float32)
        square = degree * degree - mfloat * mfloat
        factor_a = jnp.sqrt((4.0 * degree * degree - 1.0) / square)
        factor_b = jnp.sqrt((2.0 * degree + 1.0) * (degree - 1.0 - mfloat) * (degree - 1.0 + mfloat) / ((2.0 * degree - 3.0) * square))
        return factor_a[:, None] * cos_lat[None, :] * current - factor_b[:, None] * previous

    def one_turn(carried, turn_idx):
        previous, current = carried
        rows_out = []
        for offset in range(unroll):
            rows_out.append(current)
            previous, current = (current, advance(previous, current, turn_idx * unroll + offset))
        stacked = jnp.stack(rows_out, axis=1)
        contrib = jnp.einsum('skr,scr->sck', stacked, inputs, precision=highest)
        return ((previous, current), contrib)
    final_state, blocks = lax.scan(one_turn, (jnp.zeros_like(start_vals), start_vals), jnp.arange(turn_count, dtype=jnp.int32))
    return blocks.transpose(1, 2, 0, 3).reshape(slot_count, col_count, MW)

def slot_table(wave_owner, owners, slot_cap):
    wave_ids = jnp.arange(MW, dtype=jnp.int32)
    same_owner = (wave_owner[None, :] == wave_owner[:, None]) & (wave_ids[None, :] < wave_ids[:, None])
    wave_rank = lax.optimization_barrier(jnp.sum(same_owner.astype(jnp.int32), axis=1))
    keyed = wave_owner * slot_cap + wave_rank
    slots = jnp.arange(owners * slot_cap, dtype=jnp.int32)
    slot_hits = keyed[None, :] == slots[:, None]
    wave_of = lax.optimization_barrier(jnp.sum(jnp.where(slot_hits, wave_ids[None, :], 0), axis=1)).astype(jnp.int32)
    slot_used = jnp.any(slot_hits, axis=1)
    return (wave_of, slot_used)

def reference(grid_fields, sun_cosine, surface_albedo, gas_absorb, solar_weight, helper_map, row_lat, wave_owner):
    lit_cols = jnp.repeat(helper_map >= 0, BLOCK, axis=1)

    def heat_row(row_args):
        humidity, sun_cos, ground = row_args
        return radiate(humidity, sun_cos, ground, gas_absorb, solar_weight)
    heating_all = lax.map(heat_row, (grid_fields[:LEV].transpose(1, 0, 2), sun_cosine, surface_albedo))
    heating_all = jnp.where(lit_cols[:, None, :], heating_all, 0.0)
    fields = jnp.concatenate([grid_fields[:LEV], grid_fields[LEV:] + heating_all.transpose(1, 0, 2)], axis=0)
    counts = (20 + 4 * jnp.minimum(row_lat, NLAT_FULL - 1 - row_lat)).astype(jnp.int32)
    colatitude = math.pi * (row_lat.astype(jnp.float32) + 0.5) / NLAT_FULL
    cos_lat = jnp.cos(colatitude)
    sin_lat = jnp.sin(colatitude)
    spectra = row_transform(fields.transpose(1, 0, 2), counts, 0)
    row_scale = 1.0 / jnp.sqrt((ROWS_T * counts).astype(jnp.float32))
    spectra = spectra * row_scale[:, None, None, None]
    inputs = spectra.transpose(3, 1, 2, 0).reshape(MW, K * 2, ROWS_T)
    wave_ids = jnp.arange(MW, dtype=jnp.int32)
    coeffs = legendre(inputs, wave_ids, cos_lat, sin_lat)
    degree_ok = wave_ids[:, None] + wave_ids[None, :] <= MW - 1
    coeffs = jnp.where(degree_ok[:, None, :], coeffs, 0.0).reshape(MW, K, 2, MW)
    wave_of, slot_used = slot_table(wave_owner, N_LAT, MCAP)
    return jnp.where(slot_used[:, None, None, None], coeffs[wave_of], 0.0)
```

```python
import math

import jax
import jax.numpy as jnp
from jax import lax
from jax.experimental import pallas as pl
from jax.experimental.pallas import tpu as pltpu
from jax.sharding import PartitionSpec as P

LEV = 4
BLOCK = 128
NLAT_FULL = 2560
MW = 1280
G = 112
K = 8
SEG_BLOCKS = 6
ROWS_DEV = 2
N_LAT = 16
N_LON = 8
DESTS = N_LAT * N_LON
PER_DEV = 15
MCAP = PER_DEV * N_LON
ROWS_T = N_LAT * ROWS_DEV
LOG2E = math.log2(math.e)

f32 = jnp.float32
bf16 = jnp.bfloat16


def iota(shape, dim):
    return lax.broadcasted_iota(jnp.int32, shape, dim)


def dot(a, b, contract=(1, 0)):
    return lax.dot_general(
        a, b, (((contract[0],), (contract[1],)), ((), ())), preferred_element_type=f32
    )


def split(x):
    high = x.astype(bf16)
    return high, (x - high.astype(f32)).astype(bf16)


def sincos_turns(frac):
    quarter = jnp.round(frac * 4.0)
    r = (frac - quarter * 0.25) * (2.0 * math.pi)
    r2 = r * r
    sin_r = r + r * r2 * (-1.0 / 6 + r2 * (1.0 / 120 + r2 * (-1.0 / 5040 + r2 * (1.0 / 362880))))
    cos_r = 1.0 + r2 * (-0.5 + r2 * (1.0 / 24 + r2 * (-1.0 / 720 + r2 * (1.0 / 40320))))
    turns = quarter.astype(jnp.int32)
    odd = (turns & 1) == 1
    cos_v = jnp.where(odd, sin_r, cos_r)
    sin_v = jnp.where(odd, cos_r, sin_r)
    cos_v = jnp.where(((turns + 1) & 2) == 2, -cos_v, cos_v)
    sin_v = jnp.where((turns & 2) == 2, -sin_v, sin_v)
    return cos_v, sin_v


def slot_of(lane_q, lane_u):
    return (lane_q // 2) * 8 + lane_u * 2 + lane_q % 2


def find_slots(owner_ref, wave_ref):
    groups = MW // 128
    hits = [
        (owner_ref[:, b * 128 : (b + 1) * 128] == iota((N_LAT, 128), 0)).astype(f32)
        for b in range(groups)
    ]
    stacked = jnp.concatenate(hits, axis=0).astype(bf16)
    before = (iota((128, 128), 0) < iota((128, 128), 1)).astype(f32).astype(bf16)
    ahead = dot(stacked, before)
    total = dot(stacked, jnp.ones((128, 128), bf16))
    carry = jnp.zeros((N_LAT, 128), f32)
    table = jnp.zeros((2 * N_LAT, 128), f32)
    for b in range(groups):
        part = slice(b * N_LAT, (b + 1) * N_LAT)
        rank = jnp.sum(hits[b] * (ahead[part] + carry), axis=0, keepdims=True)
        carry = carry + total[part]
        ranked = (rank.astype(jnp.int32) == iota((128, 128), 0)).astype(f32).astype(bf16)
        number = iota((N_LAT, 128), 1) + (b * 128 + 1)
        high = ((number >> 4) << 4).astype(f32)
        low = (number & 15).astype(f32)
        both = jnp.concatenate([hits[b] * high, hits[b] * low], axis=0).astype(bf16)
        table = table + dot(both, ranked, (1, 1))
    table = table.astype(bf16)
    lane = iota((128, 128), 1)
    for u in range(4):
        index = slot_of(lane % 4, u)
        rank = ((lane // 4) % N_LON) * PER_DEV + index
        pick = ((iota((128, 128), 0) == rank) & (index < PER_DEV)).astype(f32).astype(bf16)
        found = dot(table, pick)
        found = found[:N_LAT] + found[N_LAT:]
        for g in range(4):
            own = iota((N_LAT, 128), 0) == g * 4 + iota((N_LAT, 128), 1) // 32
            wave_ref[u * 4 + g : u * 4 + g + 1, :] = jnp.sum(
                jnp.where(own, found, 0.0), axis=0, keepdims=True
            )


def front_kernel(
    fields_ref, sun_ref, ground_ref, gas_ref, weight_ref, lit_ref, row_ref, owner_ref,
    out_ref, wave_ref, gas_s, weight_s, left_s, spec_s,
):
    lat_me = lax.axis_index("lat")
    lon_me = lax.axis_index("lon")
    find_slots(owner_ref, wave_ref)

    def column(row):
        padded = jnp.concatenate([row, jnp.zeros((1, 128 - G), f32)], axis=1)
        return jnp.broadcast_to(padded, (128, 128)).T

    total_weight = jnp.sum(weight_ref[...], axis=1, keepdims=True)
    gas_s[...] = column(gas_ref[...])
    weight_s[...] = column(weight_ref[...] * (heat_gain / total_weight))

    counts = []
    for g in range(ROWS_DEV):
        row = row_ref[lat_me * ROWS_DEV + g]
        counts.append(20 + 4 * jnp.minimum(row, NLAT_FULL - 1 - row))

    for g in range(ROWS_DEV):

        def heat_block(a, carry, g=g):
            columns = pl.ds(pl.multiple_of(a * BLOCK, BLOCK), BLOCK)
            x = fields_ref[:, g, columns]
            depth = jnp.maximum(x, 0.0) + jnp.log1p(jnp.exp(-jnp.abs(x)))
            sun = sun_ref[g : g + 1, columns]
            slant = depth * (-LOG2E / sun)
            diffuse = depth * (-LOG2E * diffusivity)
            tile = lambda row: jnp.broadcast_to(row, (8, BLOCK))
            sun_b = tile(sun)
            ground_b = tile(ground_ref[g : g + 1, columns])
            slants = [tile(slant[level : level + 1]) for level in range(LEV)]
            diffuses = [tile(diffuse[level : level + 1]) for level in range(LEV)]
            sums = [jnp.zeros((8, BLOCK), f32) for _ in range(LEV)]
            for part in range(G // 8):
                gas = gas_s[part * 8 : (part + 1) * 8, :]
                weight = weight_s[part * 8 : (part + 1) * 8, :]
                direct, down = sun_b, None
                lost, sources, downs, passed = [], [], [], []
                for level in range(LEV):
                    t_dir = jnp.exp2(gas * slants[level])
                    t_dif = jnp.exp2(gas * diffuses[level])
                    absorbed = direct * (1.0 - t_dir)
                    source = scatter_share * absorbed
                    lost.append(absorbed)
                    sources.append(source)
                    downs.append(down)
                    passed.append(t_dif)
                    down = source if down is None else down * t_dif + source
                    direct = direct * t_dir
                upward = ground_b * (direct + down)
                for level in range(LEV - 1, -1, -1):
                    both = upward if downs[level] is None else downs[level] + upward
                    net = (1.0 - 2.0 * scatter_share) * lost[level] + (1.0 - passed[level]) * both
                    sums[level] = sums[level] + weight * net
                    upward = upward * passed[level] + sources[level]
            is_lit = lit_ref[g, a] >= 0
            heated = x
            for level in range(LEV):
                heat = jnp.where(is_lit, jnp.sum(sums[level], axis=0, keepdims=True), 0.0)
                heated = heated + jnp.where(iota((8, BLOCK), 0) == LEV + level, heat, 0.0)
            first = (lon_me * SEG_BLOCKS + a) * BLOCK
            heated = jnp.where(iota((8, BLOCK), 1) + first < counts[g], heated, 0.0)
            left_s[g, pl.ds(pl.multiple_of(a * 8, 8), 8), :] = heated
            return carry

        lax.fori_loop(0, SEG_BLOCKS, heat_block, 0)

    lefts = []
    for g in range(ROWS_DEV):
        high, low = split(left_s[g])
        top = jnp.concatenate([high, high], axis=1)
        bottom = jnp.concatenate([low, jnp.zeros_like(low)], axis=1)
        lefts.append(jnp.concatenate([top, bottom], axis=0))

    sub = iota((8, 128), 0)
    first_block = (lon_me * SEG_BLOCKS * BLOCK).astype(f32)
    steps = jnp.concatenate(
        [
            sub.astype(f32),
            (sub * 8).astype(f32),
            (sub * 8 + 64).astype(f32),
            (sub * BLOCK).astype(f32) + first_block,
        ],
        axis=0,
    )

    def transform(index, carry):
        wave = jnp.maximum(wave_ref[pl.ds(index, 1), :] - 1.0, 0.0)
        u = index // 4
        lanes = pl.ds(pl.multiple_of((index % 4) * 128, 128), 128)
        for g in range(ROWS_DEV):
            n = jnp.full((8, 128), counts[g], jnp.int32).astype(f32)
            inverse = 1.0 / n
            n_row, inverse_row = n[:1], inverse[:1]
            phase = steps * wave
            phase = phase - n_row * jnp.round(phase * inverse_row)
            cos_v, sin_v = sincos_turns(phase * inverse_row)
            cos_low, sin_low = cos_v[:8], sin_v[:8]
            highs, lows = [], []
            cos_h, cos_l, sin_h, sin_l = [], [], [], []
            for b in range(8):
                cos_p, sin_p = [], []
                for half in range(2):
                    at = 8 + b * 2 + half
                    cos_b, sin_b = cos_v[at : at + 1], sin_v[at : at + 1]
                    cos_p.append(cos_low * cos_b - sin_low * sin_b)
                    sin_p.append(sin_low * cos_b + cos_low * sin_b)
                high, low = split(jnp.concatenate(cos_p, axis=0))
                cos_h.append(high)
                cos_l.append(low)
                high, low = split(jnp.concatenate(sin_p, axis=0))
                sin_h.append(high)
                sin_l.append(low)
            right = jnp.concatenate(
                [
                    jnp.concatenate(cos_h + cos_l, axis=0),
                    jnp.concatenate(sin_h + sin_l, axis=0),
                ],
                axis=1,
            )
            both = dot(lefts[g], right)
            size = SEG_BLOCKS * 8
            both = both[:size] + both[size:]
            scale = lax.rsqrt(n_row * ROWS_T)
            cos_t, sin_t = cos_v[24:] * scale, sin_v[24:] * scale
            real = jnp.zeros((8, 128), f32)
            imag = jnp.zeros((8, 128), f32)
            for a in range(SEG_BLOCKS):
                c = both[a * 8 : a * 8 + 8, :128]
                s = both[a * 8 : a * 8 + 8, 128:]
                cos_a, sin_a = cos_t[a : a + 1], sin_t[a : a + 1]
                real = real + (cos_a * c - sin_a * s)
                imag = imag - (cos_a * s + sin_a * c)
            at = pl.multiple_of(u * 32 + g * 16, 16)
            spec_s[pl.ds(at, 16), lanes] = jnp.concatenate([real, imag], axis=0)
        return carry

    lax.fori_loop(0, 16, transform, 0)
    for g in range(4):
        out_ref[g * 128 : (g + 1) * 128, :] = spec_s[:, g * 128 : (g + 1) * 128].T


def recur_kernel(wave_ref, row_ref, high_ref, low_ref, poly_s):
    lat_me = lax.axis_index("lat")
    lon_me = lax.axis_index("lon")
    me = lat_me * N_LON + lon_me
    group = me // 32
    lane = iota((1, 128), 1)
    rows = jnp.zeros((1, 128), jnp.int32)
    for part in range(ROWS_DEV):
        for lat in range(N_LAT):
            rows = jnp.where(lane % 32 == part * 16 + lat, row_ref[lat * 2 + part], rows)
    angle = (NLAT_FULL / 2 - 0.5) - rows.astype(f32)
    _, x = sincos_turns(jnp.broadcast_to(angle * (1.0 / (2 * NLAT_FULL)), (4, 128)))
    log_sin = 0.5 * jnp.log1p(-x * x)

    found = []
    for q in range(4):
        total = jnp.zeros((1, 128), f32)
        for u in range(4):
            mine = wave_ref[pl.ds(u * 4 + group, 1), :]
            value = jnp.sum(
                jnp.where(lane == (me % 32) * 4 + q, mine, 0.0), axis=1, keepdims=True
            )
            total = jnp.where(lane // 32 == u, value, total)
        found.append(total)
    number = jnp.concatenate(found, axis=0)
    m = jnp.maximum(number - 1.0, 0.0)
    limit = jnp.where(number > 0.5, MW - m, 0.0)

    z = m + 1.0
    ratio = (z * (z + 1.0) * (z + 2.0) * (z + 3.0)) / (
        (z + 0.5) * (z + 1.5) * (z + 2.5) * (z + 3.5)
    )
    far = 1.0 / (z + 4.0)
    far2 = far * far
    log_ratio = (
        0.5 * jnp.log(z + 4.0)
        + far * (-1.0 / 8 + far2 * (1.0 / 192 - far2 * (1.0 / 640)))
        + jnp.log(ratio)
    )
    log_start = 0.5 * (
        log_ratio - math.lgamma(1.5) + jnp.where(m > 0.5, math.log(2.0), 0.0)
    )
    start = jnp.exp(log_start + m * log_sin)
    twice = 2.0 * m

    unroll = 16

    def turn(t, state):
        previous, current, shrink = state
        base = (t * unroll).astype(f32)
        for j in range(unroll):
            poly_s[pl.ds(pl.multiple_of(t * (unroll * 4), unroll * 4) + j * 4, 4), :] = current
            step = base + (j + 1.0)
            reach = twice + step
            degree2 = reach + step
            square = degree2 * degree2 - 1.0
            gap = step * reach
            root = lax.rsqrt(square * gap)
            grow = square * root
            previous, current = (
                current,
                (grow * x) * current - (grow * shrink) * previous,
            )
            shrink = gap * root
        return previous, current, shrink

    zero = jnp.zeros((4, 128), f32)
    lax.fori_loop(0, MW // unroll, turn, (zero, start, zero))

    for q in range(4):
        for b in range(MW // 128):
            piece = poly_s[pl.ds(b * 512 + q, 128, stride=4), :]
            within = (iota((128, 128), 0) + b * 128).astype(f32) < limit[q : q + 1]
            piece = jnp.where(within, piece, 0.0).T
            high, low = split(piece)
            high_ref[q * 128 : (q + 1) * 128, b * 128 : (b + 1) * 128] = high
            low_ref[q * 128 : (q + 1) * 128, b * 128 : (b + 1) * 128] = low


def back_kernel(in_ref, high_ref, low_ref, out_ref, sum_s):
    for lat in range(N_LAT):
        total = in_ref[lat * 32 : lat * 32 + 8, :]
        for part in range(1, 4):
            total = total + in_ref[lat * 32 + part * 8 : lat * 32 + part * 8 + 8, :]
        sum_s[lat * 8 : lat * 8 + 8, :] = total
    lane = iota((16, 128), 1)
    for pair in range(2):
        rows = []
        for half in range(2):
            q = pair * 2 + half
            x = sum_s[pl.ds(q, 16, stride=8), :] + sum_s[pl.ds(q + 4, 16, stride=8), :]
            for u in range(4):
                for part in range(ROWS_DEV):
                    shift = ((half - part) * 16) % 128
                    moved = x if shift == 0 else pltpu.roll(x, shift, 1)
                    at = u * 32 + half * 16
                    rows.append(jnp.where((lane >= at) & (lane < at + 16), moved, 0.0))
        first = jnp.concatenate(rows[:8], axis=0).T
        second = jnp.concatenate(rows[8:], axis=0).T
        high, low = split(jnp.concatenate([first, second], axis=1))
        left = jnp.concatenate([high, low], axis=0)
        for b in range(MW // 256):
            lanes = slice(b * 256, (b + 1) * 256)
            both = dot(left, high_ref[pair * 256 : (pair + 1) * 256, lanes])
            value = both[:128] + both[128:]
            value = value + dot(high, low_ref[pair * 256 : (pair + 1) * 256, lanes])
            for s in range(8):
                slot = pair * 8 + s
                if slot >= PER_DEV:
                    continue
                for part in range(2):
                    for t in range(2):
                        at = (slot * 8 * 10 + b * 2 + t) * 2 + part
                        out_ref[pl.ds(at, 8, stride=20), :] = value[
                            s * 16 + part * 8 : s * 16 + part * 8 + 8, t * 128 : (t + 1) * 128
                        ]


diffusivity = 1.66
scatter_share = 0.2
heat_gain = 10.0


def shards(
    grid_fields, sun_cosine, surface_albedo, gas_absorb, solar_weight, helper_map, row_lat, wave_owner
):
    vmem = pl.BlockSpec(memory_space=pltpu.VMEM)
    smem = pl.BlockSpec(memory_space=pltpu.SMEM)
    outgoing, waves = pl.pallas_call(
        front_kernel,
        out_shape=(
            jax.ShapeDtypeStruct((DESTS * 4, 128), f32),
            jax.ShapeDtypeStruct((16, 128), f32),
        ),
        in_specs=[vmem, vmem, vmem, vmem, vmem, smem, smem, vmem],
        out_specs=(vmem, vmem),
        scratch_shapes=[
            pltpu.VMEM((128, 128), f32),
            pltpu.VMEM((128, 128), f32),
            pltpu.VMEM((ROWS_DEV, SEG_BLOCKS * 8, 128), f32),
            pltpu.VMEM((128, 512), f32),
        ],
        cost_estimate=pl.CostEstimate(flops=2 * 10**8, bytes_accessed=10**6, transcendentals=10**6),
        name="front",
    )(
        grid_fields,
        sun_cosine,
        surface_albedo,
        gas_absorb.reshape(1, G),
        solar_weight.reshape(1, G),
        helper_map,
        row_lat,
        wave_owner.reshape(1, MW),
    )
    incoming = lax.all_to_all(
        outgoing.reshape(DESTS, 4, 128), ("lat", "lon"), split_axis=0, concat_axis=0, tiled=True
    )
    high, low = pl.pallas_call(
        recur_kernel,
        out_shape=(
            jax.ShapeDtypeStruct((512, MW), bf16),
            jax.ShapeDtypeStruct((512, MW), bf16),
        ),
        in_specs=[vmem, smem],
        out_specs=(vmem, vmem),
        scratch_shapes=[pltpu.VMEM((MW * 4, 128), f32)],
        cost_estimate=pl.CostEstimate(flops=2 * 10**7, bytes_accessed=3 * 10**6, transcendentals=10**6),
        name="recur",
    )(waves, row_lat)
    rows = pl.pallas_call(
        back_kernel,
        out_shape=jax.ShapeDtypeStruct((PER_DEV * K * 10 * 2, 128), f32),
        in_specs=[vmem, vmem, vmem],
        out_specs=vmem,
        scratch_shapes=[pltpu.VMEM((128, 128), f32)],
        cost_estimate=pl.CostEstimate(flops=5 * 10**8, bytes_accessed=4 * 10**6, transcendentals=0),
        name="back",
    )(incoming.reshape(DESTS * 4, 128), high, low)
    return (
        rows.reshape(PER_DEV, K, 10, 2, 128).transpose(0, 1, 3, 2, 4).reshape(PER_DEV, K, 2, MW)
    )


def solution(mesh):
    placed = (
        P(None, "lat", "lon"),
        P("lat", "lon"),
        P("lat", "lon"),
        P(),
        P(),
        P("lat", "lon"),
        P(),
        P(),
    )
    return jax.shard_map(
        shards,
        mesh=mesh,
        in_specs=placed,
        out_specs=P(("lat", "lon"), None, None, None),
        check_vma=False,
    )
```

```python
import math

import jax
import jax.numpy as jnp
from jax import lax
from jax.experimental import pallas as pl
from jax.experimental.pallas import tpu as pltpu
from jax.sharding import PartitionSpec as P

LEV = 4
BLOCK = 128
NLAT_FULL = 2560
MW = 1280
G = 112
K = 8
SEG_BLOCKS = 6
ROWS_DEV = 2
N_LAT = 16
N_LON = 8
DESTS = N_LAT * N_LON
PER_DEV = 15
MCAP = PER_DEV * N_LON
ROWS_T = N_LAT * ROWS_DEV
LOG2E = math.log2(math.e)

f32 = jnp.float32
bf16 = jnp.bfloat16


def iota(shape, dim):
    return lax.broadcasted_iota(jnp.int32, shape, dim)


def dot(a, b, contract=(1, 0)):
    return lax.dot_general(
        a, b, (((contract[0],), (contract[1],)), ((), ())), preferred_element_type=f32
    )


def split(x):
    high = x.astype(bf16)
    return high, (x - high.astype(f32)).astype(bf16)


def sincos_quarter(r):
    r2 = r * r
    sin_v = r + (r * r2) * (-1.6666654611e-1 + r2 * (8.3321608736e-3 - r2 * 1.9515295891e-4))
    cos_v = 1.0 + r2 * (
        -0.5 + r2 * (4.166664568298827e-2 + r2 * (-1.388731625493765e-3 + r2 * 2.443315711809948e-5))
    )
    for _ in range(2):
        twice = sin_v + sin_v
        cos_v, sin_v = 1.0 - twice * sin_v, twice * cos_v
    return cos_v, sin_v


def slot_of(lane_q, lane_u):
    return (lane_q // 2) * 8 + lane_u * 2 + lane_q % 2


def slot_picks(pick_ref):
    lane = iota((128, 128), 1)
    for u in range(4):
        index = slot_of(lane % 4, u)
        rank = ((lane // 4) % N_LON) * PER_DEV + index
        pick = (iota((128, 128), 0) == rank) & (index < PER_DEV)
        pick_ref[u] = pick.astype(f32).astype(bf16)


def find_slots(owner_ref, pick_ref, wave_ref):
    groups = MW // 128
    hits = [
        (owner_ref[b : b + 1, :] == iota((N_LAT, 128), 0)).astype(f32) for b in range(groups)
    ]
    stacked = jnp.concatenate(hits, axis=0).astype(bf16)
    before = (iota((128, 128), 0) < iota((128, 128), 1)).astype(f32).astype(bf16)
    ahead = dot(stacked, before)
    total = dot(stacked, jnp.ones((128, 128), bf16))
    carry = jnp.zeros((N_LAT, 128), f32)
    table = jnp.zeros((2 * N_LAT, 128), f32)
    for b in range(groups):
        part = slice(b * N_LAT, (b + 1) * N_LAT)
        rank = jnp.sum(hits[b] * (ahead[part] + carry), axis=0, keepdims=True)
        carry = carry + total[part]
        ranked = (rank.astype(jnp.int32) == iota((128, 128), 0)).astype(f32).astype(bf16)
        number = iota((N_LAT, 128), 1) + (b * 128 + 1)
        high = ((number >> 4) << 4).astype(f32)
        low = (number & 15).astype(f32)
        both = jnp.concatenate([hits[b] * high, hits[b] * low], axis=0).astype(bf16)
        table = table + dot(both, ranked, (1, 1))
    table = table.astype(bf16)
    for u in range(4):
        found = dot(table, pick_ref[u])
        found = found[:N_LAT] + found[N_LAT:]
        for g in range(4):
            own = iota((N_LAT, 128), 0) == g * 4 + iota((N_LAT, 128), 1) // 32
            wave_ref[u * 4 + g : u * 4 + g + 1, :] = jnp.sum(
                jnp.where(own, found, 0.0), axis=0, keepdims=True
            )


def front_kernel(
    fields_hbm, sun_hbm, ground_hbm, gas_hbm, weight_hbm, lit_hbm, row_hbm, owner_hbm,
    out_hbm, wave_ref,
    fields_ref, sun_ref, ground_ref, gas_ref, weight_ref, lit_ref, row_ref, owner_ref,
    out_s, pick_s, gas_s, weight_s, left_s, spec_s, turn_s, in_sems, out_sems,
):
    lat_me = lax.axis_index("lat")
    lon_me = lax.axis_index("lon")
    pairs = [
        (owner_hbm, owner_ref),
        (gas_hbm, gas_ref),
        (weight_hbm, weight_ref),
        (row_hbm, row_ref),
        (lit_hbm, lit_ref),
        (sun_hbm, sun_ref),
        (ground_hbm, ground_ref),
    ] + [(fields_hbm.at[:, g, :], fields_ref.at[g]) for g in range(ROWS_DEV)]
    arrivals = [
        pltpu.make_async_copy(source, target, in_sems.at[index])
        for index, (source, target) in enumerate(pairs)
    ]
    for copy in arrivals:
        copy.start()
    slot_picks(pick_s)
    arrivals[0].wait()
    find_slots(owner_ref, pick_s, wave_ref)
    for copy in arrivals[1:]:
        copy.wait()

    def column(row):
        padded = jnp.concatenate([row, jnp.zeros((1, 128 - G), f32)], axis=1)
        return jnp.broadcast_to(padded, (128, 128)).T

    total_weight = jnp.sum(weight_ref[...], axis=1, keepdims=True)
    gas_s[...] = column(gas_ref[...])
    weight_s[...] = column(weight_ref[...] * (heat_gain / total_weight))

    counts = []
    for g in range(ROWS_DEV):
        row = row_ref[lat_me * ROWS_DEV + g]
        counts.append(20 + 4 * jnp.minimum(row, NLAT_FULL - 1 - row))

    for g in range(ROWS_DEV):

        def heat_block(a, carry, g=g):
            columns = pl.ds(pl.multiple_of(a * BLOCK, BLOCK), BLOCK)
            x = fields_ref[g, :, columns]
            depth = jnp.maximum(x, 0.0) + jnp.log1p(jnp.exp(-jnp.abs(x)))
            sun = sun_ref[g : g + 1, columns]
            slant = depth * (-LOG2E / sun)
            diffuse = depth * (-LOG2E * diffusivity)
            tile = lambda row: jnp.broadcast_to(row, (8, BLOCK))
            sun_b = tile(sun * scatter_share)
            ground = ground_ref[g : g + 1, columns]
            ground_b = tile(ground)
            slants = [tile(slant[level : level + 1]) for level in range(LEV)]
            diffuses = [tile(diffuse[level : level + 1]) for level in range(LEV)]
            nets = [jnp.zeros((8, BLOCK), f32) for _ in range(LEV + 1)]
            beams = [jnp.zeros((8, BLOCK), f32) for _ in range(LEV + 1)]
            for part in range(G // 8):
                gas = gas_s[part * 8 : (part + 1) * 8, :]
                beam = sun_b * weight_s[part * 8 : (part + 1) * 8, :]
                beams[0] = beams[0] + beam
                down, downs, sources, passed = None, [], [], []
                for level in range(LEV):
                    after = beam * jnp.exp2(gas * slants[level])
                    source = beam - after
                    beam = after
                    t_dif = jnp.exp2(gas * diffuses[level])
                    down = source if down is None else down * t_dif + source
                    beams[level + 1] = beams[level + 1] + beam
                    downs.append(down)
                    sources.append(source)
                    passed.append(t_dif)
                nets[LEV] = nets[LEV] + down
                upward = ground_b * (beam * (1.0 / scatter_share) + down)
                for level in range(LEV - 1, -1, -1):
                    upward = upward * passed[level] + sources[level]
                    if level:
                        nets[level] = nets[level] + (downs[level - 1] - upward)
                    else:
                        nets[level] = nets[level] - upward
            nets = [net + beams[level] * (1.0 / scatter_share) for level, net in enumerate(nets)]
            nets[LEV] = nets[LEV] * (1.0 - ground)
            sums = [nets[level] - nets[level + 1] for level in range(LEV)]
            is_lit = lit_ref[g, a] >= 0
            heated = x
            for level in range(LEV):
                heat = jnp.where(is_lit, jnp.sum(sums[level], axis=0, keepdims=True), 0.0)
                heated = heated + jnp.where(iota((8, BLOCK), 0) == LEV + level, heat, 0.0)
            first = (lon_me * SEG_BLOCKS + a) * BLOCK
            heated = jnp.where(iota((8, BLOCK), 1) + first < counts[g], heated, 0.0)
            left_s[g, pl.ds(pl.multiple_of(a * 8, 8), 8), :] = heated
            return carry

        lax.fori_loop(0, SEG_BLOCKS, heat_block, 0)

    offset, place = iota((BLOCK, BLOCK), 0), iota((BLOCK, BLOCK), 1)
    half = BLOCK // 2
    step = place % half
    fold = jnp.where(offset == half + step, 1.0, 0.0)
    mirror = jnp.where(offset == half - 1 - step, 1.0, 0.0)
    fold = (fold + jnp.where(place < half, mirror, -mirror)).astype(bf16)
    size = SEG_BLOCKS * 8
    is_even = iota((size, BLOCK), 1) < half
    lefts = []
    for g in range(ROWS_DEV):
        x = left_s[g]
        first = x.astype(bf16)
        second, third = split(x - first.astype(f32))
        folded = dot(jnp.concatenate([first, second, third], axis=0), fold)
        folded = folded[:size] + (folded[size : 2 * size] + folded[2 * size :])
        evens = split(jnp.where(is_even, folded, 0.0))
        odds = split(jnp.where(is_even, 0.0, folded))
        empty = jnp.zeros((size, BLOCK), bf16)
        lefts.append(
            jnp.concatenate(
                [
                    jnp.concatenate([evens[0], evens[0]], axis=1),
                    jnp.concatenate([odds[0], odds[0]], axis=1),
                    jnp.concatenate([evens[1], empty], axis=1),
                    jnp.concatenate([odds[1], empty], axis=1),
                ],
                axis=0,
            )
        )

    sub = iota((8, 128), 0)
    first_block = (lon_me * SEG_BLOCKS * 2 * BLOCK).astype(f32)
    steps = jnp.concatenate(
        [
            (sub * 2 + 1).astype(f32),
            (sub * 16).astype(f32),
            (sub * (2 * BLOCK) + (BLOCK - 1)).astype(f32) + first_block,
        ],
        axis=0,
    )
    steps = jnp.where(iota((24, 128), 0) < 16 + SEG_BLOCKS, steps, 0.0)
    departures = []
    for lat_group in range(4):
        lanes = slice(lat_group * 128, (lat_group + 1) * 128)
        for pair in range(2):
            for g in range(ROWS_DEV):
                n = jnp.full((1, 128), counts[g] * 2, jnp.int32).astype(f32)
                inverse = 1.0 / n
                scale = lax.rsqrt(n * (ROWS_T / 2))
                rights = []
                for u in (pair * 2, pair * 2 + 1):
                    index = u * 4 + lat_group
                    wave = jnp.maximum(wave_ref[index : index + 1, :] - 1.0, 0.0)
                    phase = steps * wave
                    phase = phase - n * jnp.round(phase * inverse)
                    cos_v, sin_v = sincos_quarter(phase * (inverse * (math.pi / 2)))
                    at = (g * 16 + index) * 32
                    turn_s[at : at + 8, :] = cos_v[8:16]
                    turn_s[at + 8 : at + 16, :] = sin_v[8:16]
                    turn_s[at + 16 : at + 24, :] = cos_v[16:] * scale
                    turn_s[at + 24 : at + 32, :] = sin_v[16:] * scale
                    cos_low, sin_low = cos_v[:8], sin_v[:8]
                    cos_h, cos_l, sin_h, sin_l = [], [], [], []
                    for b in range(0, 8, 2):
                        cos_p, sin_p = [], []
                        for r in (b, b + 1):
                            cos_r = turn_s[pl.ds(at + r, 8, stride=0), :]
                            sin_r = turn_s[pl.ds(at + 8 + r, 8, stride=0), :]
                            cos_p.append(cos_low * cos_r - sin_low * sin_r)
                            sin_p.append(sin_low * cos_r + cos_low * sin_r)
                        high, low = split(jnp.concatenate(cos_p, axis=0))
                        cos_h.append(high)
                        cos_l.append(low)
                        high, low = split(jnp.concatenate(sin_p, axis=0))
                        sin_h.append(high)
                        sin_l.append(low)
                    rights.append(jnp.concatenate(cos_h + sin_h + cos_l + sin_l, axis=0))
                both = dot(lefts[g], jnp.concatenate(rights, axis=1))
                both = both[: 2 * size] + both[2 * size :]
                for k in range(2):
                    u = pair * 2 + k
                    at = (g * 16 + u * 4 + lat_group) * 32
                    real = jnp.zeros((8, 128), f32)
                    imag = jnp.zeros((8, 128), f32)
                    for a in range(SEG_BLOCKS):
                        c = both[a * 8 : a * 8 + 8, k * 128 : (k + 1) * 128]
                        s = both[size + a * 8 : size + a * 8 + 8, k * 128 : (k + 1) * 128]
                        cos_a = turn_s[pl.ds(at + 16 + a, 8, stride=0), :]
                        sin_a = turn_s[pl.ds(at + 24 + a, 8, stride=0), :]
                        real = real + (cos_a * c - sin_a * s)
                        imag = imag - (cos_a * s + sin_a * c)
                    row = u * 32 + g * 16
                    spec_s[row : row + 16, lanes] = jnp.concatenate([real, imag], axis=0)
        out_s[lanes, :] = spec_s[:, lanes].T
        copy = pltpu.make_async_copy(out_s.at[lanes, :], out_hbm.at[lanes, :], out_sems.at[lat_group])
        copy.start()
        departures.append(copy)
    for copy in departures:
        copy.wait()


def recur_kernel(wave_ref, row_ref, high_ref, low_ref, poly_s):
    lat_me = lax.axis_index("lat")
    lon_me = lax.axis_index("lon")
    me = lat_me * N_LON + lon_me
    group = me // 32
    lane = iota((1, 128), 1)
    rows = jnp.zeros((1, 128), jnp.int32)
    for part in range(ROWS_DEV):
        for lat in range(N_LAT):
            rows = jnp.where(lane % 32 == part * 16 + lat, row_ref[lat * 2 + part], rows)
    angle = (NLAT_FULL / 2 - 0.5) - rows.astype(f32)
    _, x = sincos_quarter(jnp.broadcast_to(angle * (math.pi / (4 * NLAT_FULL)), (4, 128)))
    log_sin = 0.5 * jnp.log1p(-x * x)

    found = []
    for q in range(4):
        total = jnp.zeros((1, 128), f32)
        for u in range(4):
            mine = wave_ref[pl.ds(u * 4 + group, 1), :]
            value = jnp.sum(
                jnp.where(lane == (me % 32) * 4 + q, mine, 0.0), axis=1, keepdims=True
            )
            total = jnp.where(lane // 32 == u, value, total)
        found.append(total)
    number = jnp.concatenate(found, axis=0)
    m = jnp.maximum(number - 1.0, 0.0)
    limit = jnp.where(number > 0.5, MW - m, 0.0)

    z = m + 1.0
    ratio = (z * (z + 1.0) * (z + 2.0) * (z + 3.0)) / (
        (z + 0.5) * (z + 1.5) * (z + 2.5) * (z + 3.5)
    )
    far = 1.0 / (z + 4.0)
    far2 = far * far
    log_ratio = (
        0.5 * jnp.log(z + 4.0)
        + far * (-1.0 / 8 + far2 * (1.0 / 192 - far2 * (1.0 / 640)))
        + jnp.log(ratio)
    )
    log_start = 0.5 * (
        log_ratio - math.lgamma(1.5) + jnp.where(m > 0.5, math.log(2.0), 0.0)
    )
    start = jnp.exp(log_start + m * log_sin)
    twice = 2.0 * m

    unroll = 16

    def turn(t, state):
        previous, current, shrink = state
        base = (t * unroll).astype(f32)
        for j in range(unroll):
            poly_s[pl.ds(pl.multiple_of(t * (unroll * 4), unroll * 4) + j * 4, 4), :] = current
            step = base + (j + 1.0)
            reach = twice + step
            degree2 = reach + step
            square = degree2 * degree2 - 1.0
            gap = step * reach
            root = lax.rsqrt(square * gap)
            grow = square * root
            previous, current = (
                current,
                (grow * x) * current - (grow * shrink) * previous,
            )
            shrink = gap * root
        return previous, current, shrink

    zero = jnp.zeros((4, 128), f32)
    lax.fori_loop(0, MW // unroll, turn, (zero, start, zero))

    for q in range(4):
        for b in range(MW // 128):
            piece = poly_s[pl.ds(b * 512 + q, 128, stride=4), :]
            within = (iota((128, 128), 0) + b * 128).astype(f32) < limit[q : q + 1]
            piece = jnp.where(within, piece, 0.0).T
            high, low = split(piece)
            high_ref[q * 128 : (q + 1) * 128, b * 128 : (b + 1) * 128] = high
            low_ref[q * 128 : (q + 1) * 128, b * 128 : (b + 1) * 128] = low


def back_kernel(in_ref, high_ref, low_ref, out_ref, sum_s, result_s, sems):
    for lat in range(N_LAT):
        total = in_ref[lat * 32 : lat * 32 + 8, :]
        for part in range(1, 4):
            total = total + in_ref[lat * 32 + part * 8 : lat * 32 + part * 8 + 8, :]
        sum_s[lat * 8 : lat * 8 + 8, :] = total
    lane = iota((16, 128), 1)
    lefts = []
    for pair in range(2):
        rows = []
        for half in range(2):
            q = pair * 2 + half
            x = sum_s[pl.ds(q, 16, stride=8), :] + sum_s[pl.ds(q + 4, 16, stride=8), :]
            for u in range(4):
                for part in range(ROWS_DEV):
                    shift = ((half - part) * 16) % 128
                    moved = x if shift == 0 else pltpu.roll(x, shift, 1)
                    at = u * 32 + half * 16
                    rows.append(jnp.where((lane >= at) & (lane < at + 16), moved, 0.0))
        first = jnp.concatenate(rows[:8], axis=0).T
        second = jnp.concatenate(rows[8:], axis=0).T
        lefts.append(split(jnp.concatenate([first, second], axis=1)))
    copies = []
    for b in range(MW // 256):
        lanes = slice(b * 256, (b + 1) * 256)
        for pair in range(2):
            high, low = lefts[pair]
            rows = slice(pair * 256, (pair + 1) * 256)
            both = dot(jnp.concatenate([high, low], axis=0), high_ref[rows, lanes])
            value = both[:128] + both[128:] + dot(high, low_ref[rows, lanes])
            for s in range(8):
                slot = pair * 8 + s
                if slot < PER_DEV:
                    for part in range(2):
                        at = s * 16 + part * 8
                        result_s[slot, :, part, lanes] = value[at : at + 8]
        copy = pltpu.make_async_copy(
            result_s.at[:, :, :, lanes], out_ref.at[:, :, :, lanes], sems.at[b]
        )
        copy.start()
        copies.append(copy)
    for copy in copies:
        copy.wait()


diffusivity = 1.66
scatter_share = 0.2
heat_gain = 10.0


def shards(
    grid_fields, sun_cosine, surface_albedo, gas_absorb, solar_weight, helper_map, row_lat, wave_owner
):
    vmem = pl.BlockSpec(memory_space=pltpu.VMEM)
    smem = pl.BlockSpec(memory_space=pltpu.SMEM)
    hbm = pl.BlockSpec(memory_space=pl.ANY)
    limits = pltpu.CompilerParams(vmem_limit_bytes=16 * 2**20)
    outgoing, waves = pl.pallas_call(
        front_kernel,
        out_shape=(
            jax.ShapeDtypeStruct((DESTS * 4, 128), f32),
            jax.ShapeDtypeStruct((16, 128), f32),
        ),
        in_specs=[hbm] * 8,
        out_specs=(hbm, vmem),
        scratch_shapes=[
            pltpu.VMEM((ROWS_DEV, K, SEG_BLOCKS * BLOCK), f32),
            pltpu.VMEM((ROWS_DEV, SEG_BLOCKS * BLOCK), f32),
            pltpu.VMEM((ROWS_DEV, SEG_BLOCKS * BLOCK), f32),
            pltpu.VMEM((1, G), f32),
            pltpu.VMEM((1, G), f32),
            pltpu.SMEM((ROWS_DEV, SEG_BLOCKS), jnp.int32),
            pltpu.SMEM((ROWS_T,), jnp.int32),
            pltpu.VMEM((MW // 128, 128), jnp.int32),
            pltpu.VMEM((DESTS * 4, 128), f32),
            pltpu.VMEM((4, 128, 128), bf16),
            pltpu.VMEM((128, 128), f32),
            pltpu.VMEM((128, 128), f32),
            pltpu.VMEM((ROWS_DEV, SEG_BLOCKS * 8, 128), f32),
            pltpu.VMEM((128, 512), f32),
            pltpu.VMEM((1024, 128), f32),
            pltpu.SemaphoreType.DMA((9,)),
            pltpu.SemaphoreType.DMA((4,)),
        ],
        cost_estimate=pl.CostEstimate(flops=2 * 10**8, bytes_accessed=10**6, transcendentals=10**6),
        name="front",
        compiler_params=pltpu.CompilerParams(vmem_limit_bytes=60 * 2**20),
    )(
        grid_fields,
        sun_cosine,
        surface_albedo,
        gas_absorb.reshape(1, G),
        solar_weight.reshape(1, G),
        helper_map,
        row_lat,
        wave_owner.reshape(MW // 128, 128),
    )
    incoming = lax.all_to_all(
        outgoing.reshape(DESTS, 4, 128), ("lat", "lon"), split_axis=0, concat_axis=0, tiled=True
    )
    high, low = pl.pallas_call(
        recur_kernel,
        out_shape=(
            jax.ShapeDtypeStruct((512, MW), bf16),
            jax.ShapeDtypeStruct((512, MW), bf16),
        ),
        in_specs=[vmem, smem],
        out_specs=(vmem, vmem),
        scratch_shapes=[pltpu.VMEM((MW * 4, 128), f32)],
        cost_estimate=pl.CostEstimate(flops=2 * 10**7, bytes_accessed=3 * 10**6, transcendentals=10**6),
        name="recur",
        compiler_params=limits,
    )(waves, row_lat)
    return pl.pallas_call(
        back_kernel,
        out_shape=jax.ShapeDtypeStruct((PER_DEV, K, 2, MW), f32),
        in_specs=[vmem, vmem, vmem],
        out_specs=pl.BlockSpec(memory_space=pl.ANY),
        scratch_shapes=[
            pltpu.VMEM((128, 128), f32),
            pltpu.VMEM((PER_DEV, K, 2, MW), f32),
            pltpu.SemaphoreType.DMA((MW // 256,)),
        ],
        cost_estimate=pl.CostEstimate(flops=5 * 10**8, bytes_accessed=4 * 10**6, transcendentals=0),
        name="back",
        compiler_params=limits,
    )(incoming.reshape(DESTS * 4, 128), high, low)


def solution(mesh):
    placed = (
        P(None, "lat", "lon"),
        P("lat", "lon"),
        P("lat", "lon"),
        P(),
        P(),
        P("lat", "lon"),
        P(),
        P(),
    )
    return jax.shard_map(
        shards,
        mesh=mesh,
        in_specs=placed,
        out_specs=P(("lat", "lon"), None, None, None),
        check_vma=False,
    )
```

```python
import math

import jax
import jax.numpy as jnp
from jax import lax
from jax.experimental import pallas as pl
from jax.experimental.pallas import tpu as pltpu
from jax.sharding import PartitionSpec as P

LEV = 4
BLOCK = 128
NLAT_FULL = 2560
MW = 1280
G = 112
K = 8
SEG_BLOCKS = 6
ROWS_DEV = 2
N_LAT = 16
N_LON = 8
DESTS = N_LAT * N_LON
PER_DEV = 15
MCAP = PER_DEV * N_LON
ROWS_T = N_LAT * ROWS_DEV
LOG2E = math.log2(math.e)

f32 = jnp.float32
bf16 = jnp.bfloat16


def iota(shape, dim):
    return lax.broadcasted_iota(jnp.int32, shape, dim)


def dot(a, b, contract=(1, 0)):
    return lax.dot_general(
        a, b, (((contract[0],), (contract[1],)), ((), ())), preferred_element_type=f32
    )


def split(x):
    high = x.astype(bf16)
    return high, (x - high.astype(f32)).astype(bf16)


def sincos_quarter(r):
    r2 = r * r
    sin_v = r + (r * r2) * (-1.6666654611e-1 + r2 * (8.3321608736e-3 - r2 * 1.9515295891e-4))
    cos_v = 1.0 + r2 * (
        -0.5 + r2 * (4.166664568298827e-2 + r2 * (-1.388731625493765e-3 + r2 * 2.443315711809948e-5))
    )
    for _ in range(2):
        twice = sin_v + sin_v
        cos_v, sin_v = 1.0 - twice * sin_v, twice * cos_v
    return cos_v, sin_v


def slot_of(lane_q, lane_u):
    return (lane_q // 2) * 8 + lane_u * 2 + lane_q % 2


def slot_picks(pick_ref):
    lane = iota((128, 128), 1)
    for u in range(4):
        index = slot_of(lane % 4, u)
        rank = ((lane // 4) % N_LON) * PER_DEV + index
        pick = (iota((128, 128), 0) == rank) & (index < PER_DEV)
        pick_ref[u] = pick.astype(f32).astype(bf16)


def find_slots(owner_ref, pick_ref, wave_ref):
    groups = MW // 128
    hits = [
        (owner_ref[b : b + 1, :] == iota((N_LAT, 128), 0)).astype(f32) for b in range(groups)
    ]
    stacked = jnp.concatenate(hits, axis=0).astype(bf16)
    before = (iota((128, 128), 0) < iota((128, 128), 1)).astype(f32).astype(bf16)
    ahead = dot(stacked, before)
    total = dot(stacked, jnp.ones((128, 128), bf16))
    carry = jnp.zeros((N_LAT, 128), f32)
    table = jnp.zeros((2 * N_LAT, 128), f32)
    for b in range(groups):
        part = slice(b * N_LAT, (b + 1) * N_LAT)
        rank = jnp.sum(hits[b] * (ahead[part] + carry), axis=0, keepdims=True)
        carry = carry + total[part]
        ranked = (rank.astype(jnp.int32) == iota((128, 128), 0)).astype(f32).astype(bf16)
        number = iota((N_LAT, 128), 1) + (b * 128 + 1)
        high = ((number >> 4) << 4).astype(f32)
        low = (number & 15).astype(f32)
        both = jnp.concatenate([hits[b] * high, hits[b] * low], axis=0).astype(bf16)
        table = table + dot(both, ranked, (1, 1))
    table = table.astype(bf16)
    for u in range(4):
        found = dot(table, pick_ref[u])
        found = found[:N_LAT] + found[N_LAT:]
        for g in range(4):
            own = iota((N_LAT, 128), 0) == g * 4 + iota((N_LAT, 128), 1) // 32
            wave_ref[u * 4 + g : u * 4 + g + 1, :] = jnp.sum(
                jnp.where(own, found, 0.0), axis=0, keepdims=True
            )


def front_kernel(
    fields_hbm, sun_hbm, ground_hbm, gas_hbm, weight_hbm, lit_hbm, row_hbm, owner_hbm,
    out_hbm, wave_hbm,
    fields_ref, sun_ref, ground_ref, gas_ref, weight_ref, lit_ref, row_ref, owner_ref,
    out_s, pick_s, share_s, beam_s, left_s, spec_s, turn_s, wave_ref, in_sems, out_sems,
):
    lat_me = lax.axis_index("lat")
    lon_me = lax.axis_index("lon")
    pairs = [
        (owner_hbm, owner_ref),
        (gas_hbm, gas_ref),
        (weight_hbm, weight_ref),
        (row_hbm, row_ref),
        (lit_hbm, lit_ref),
        (sun_hbm, sun_ref),
        (ground_hbm, ground_ref),
    ] + [(fields_hbm.at[:, g, :], fields_ref.at[g]) for g in range(ROWS_DEV)]
    arrivals = [
        pltpu.make_async_copy(source, target, in_sems.at[index])
        for index, (source, target) in enumerate(pairs)
    ]
    for copy in arrivals:
        copy.start()
    slot_picks(pick_s)
    arrivals[0].wait()
    for copy in arrivals[1:]:
        copy.wait()
    find_slots(owner_ref, pick_s, wave_ref)
    departures = [pltpu.make_async_copy(wave_ref, wave_hbm, out_sems.at[4])]
    departures[0].start()

    def column(row):
        padded = jnp.concatenate([row, jnp.ones((1, 128 - G), f32)], axis=1)
        return jnp.broadcast_to(padded, (128, 128)).T

    def thirds(x):
        first = x.astype(bf16).astype(f32)
        second = (x - first).astype(bf16).astype(f32)
        return first, second, (x - first - second).astype(bf16).astype(f32)

    kinds = 2 * LEV
    total_weight = jnp.sum(weight_ref[...], axis=1, keepdims=True)
    gas = column(gas_ref[...])
    share = column(weight_ref[...] * (heat_gain / total_weight))
    beam_s[...] = share
    gas_1, gas_2, gas_3 = thirds(gas)
    log_1, log_2, log_3 = thirds(jnp.log2(share))
    lane = iota((8, 128), 1)
    term = lane // kinds
    for part in range(G // 8):
        rows = slice(part * 8, (part + 1) * 8)
        factor = jnp.where(
            (term == 1) | (term == 4), gas_2[rows], jnp.where(term == 2, gas_3[rows], gas_1[rows])
        )
        tail = jnp.where(
            lane < 6 * kinds + 3,
            1.0,
            jnp.where(
                lane == 6 * kinds + 3,
                log_1[rows],
                jnp.where(lane == 6 * kinds + 4, log_2[rows], log_3[rows]),
            ),
        )
        tail = jnp.where((term == 6) & (lane < 6 * kinds + 6), tail, 0.0)
        pieces = []
        for kind in range(kinds):
            own = jnp.where((lane % kinds == kind) & (term < 6), factor, 0.0)
            pieces.append(jnp.where(term == 6, tail, own) if kind < LEV else own)
        share_s[part * 64 : (part + 1) * 64, :] = jnp.concatenate(pieces, axis=0).astype(bf16)

    counts = []
    for g in range(ROWS_DEV):
        row = row_ref[lat_me * ROWS_DEV + g]
        counts.append(20 + 4 * jnp.minimum(row, NLAT_FULL - 1 - row))

    sub = iota((8, BLOCK), 0)
    tile = lambda row: jnp.broadcast_to(row, (8, BLOCK))
    for a in range(SEG_BLOCKS):
        columns = slice(a * BLOCK, (a + 1) * BLOCK)
        paths, grounds, suns = [], [], []
        for g in range(ROWS_DEV):
            x = fields_ref[g, :, columns]
            depth = jnp.maximum(x, 0.0) + jnp.log1p(jnp.exp(-jnp.abs(x)))
            sun = sun_ref[g : g + 1, columns]
            suns.append(sun)
            grounds.append(ground_ref[g : g + 1, columns])
            slant = tile(depth[:1])
            for level in range(1, LEV):
                slant = slant + jnp.where(sub >= level, tile(depth[level : level + 1]), 0.0)
            path = jnp.where(
                sub < LEV,
                slant * (-LOG2E / sun),
                pltpu.roll(depth, LEV, 0) * (-LOG2E * diffusivity),
            )
            path_1, path_2, path_3 = thirds(path)
            logs = thirds(tile(jnp.log2(sun * scatter_share)))
            tail = jnp.where(
                sub == 0, logs[0], jnp.where(sub == 1, logs[1], jnp.where(sub == 2, logs[2], 1.0))
            )
            zero = jnp.zeros((8, BLOCK), f32)
            stack = [path_1, path_1, path_1, path_2, path_2, path_3, tail] + [zero] * 9
            paths.append(jnp.concatenate(stack, axis=0).astype(bf16))
        right = jnp.concatenate(paths, axis=1)
        nets = [[jnp.zeros((8, BLOCK), f32) for _ in range(LEV + 1)] for _ in range(ROWS_DEV)]
        beams = [[jnp.zeros((8, BLOCK), f32) for _ in range(LEV + 1)] for _ in range(ROWS_DEV)]
        for g in range(ROWS_DEV):
            beams[g][0] = tile(suns[g] * (scatter_share * heat_gain / 8))
        ground_b = [tile(ground) for ground in grounds]
        sun_b = [tile(sun * scatter_share) for sun in suns]
        for part in range(G // 8):
            passing = jnp.exp2(dot(share_s[part * 64 : (part + 1) * 64, :], right))
            for g in range(ROWS_DEV):
                net, beam_sum = nets[g], beams[g]
                pick = lambda kind: passing[kind * 8 : kind * 8 + 8, g * BLOCK : (g + 1) * BLOCK]
                beam = sun_b[g] * beam_s[part * 8 : (part + 1) * 8, :]
                down, downs, sources = None, [], []
                for level in range(LEV):
                    after = pick(level)
                    source = beam - after
                    beam = after
                    down = source if down is None else down * pick(LEV + level) + source
                    beam_sum[level + 1] = beam_sum[level + 1] + beam
                    downs.append(down)
                    sources.append(source)
                net[LEV] = net[LEV] + down
                upward = ground_b[g] * (beam * (1.0 / scatter_share) + down)
                for level in range(LEV - 1, -1, -1):
                    upward = upward * pick(LEV + level) + sources[level]
                    if level:
                        net[level] = net[level] + (downs[level - 1] - upward)
                    else:
                        net[level] = net[level] - upward
        for g in range(ROWS_DEV):
            levels = [
                net + beam_sum * (1.0 / scatter_share) for net, beam_sum in zip(nets[g], beams[g])
            ]
            levels[LEV] = levels[LEV] * (1.0 - grounds[g])
            is_lit = lit_ref[g, a] >= 0
            heated = fields_ref[g, :, columns]
            for level in range(LEV):
                heat = jnp.sum(levels[level] - levels[level + 1], axis=0, keepdims=True)
                heat = jnp.where(is_lit, heat, 0.0)
                heated = heated + jnp.where(sub == LEV + level, heat, 0.0)
            first = (lon_me * SEG_BLOCKS + a) * BLOCK
            heated = jnp.where(iota((8, BLOCK), 1) + first < counts[g], heated, 0.0)
            left_s[g, a * 8 : (a + 1) * 8, :] = heated

    offset, place = iota((BLOCK, BLOCK), 0), iota((BLOCK, BLOCK), 1)
    half = BLOCK // 2
    step = place % half
    fold = jnp.where(offset == half + step, 1.0, 0.0)
    mirror = jnp.where(offset == half - 1 - step, 1.0, 0.0)
    fold = (fold + jnp.where(place < half, mirror, -mirror)).astype(bf16)
    size = SEG_BLOCKS * 8
    is_even = iota((size, BLOCK), 1) < half
    lefts = []
    for g in range(ROWS_DEV):
        x = left_s[g]
        first = x.astype(bf16)
        second, third = split(x - first.astype(f32))
        folded = dot(jnp.concatenate([first, second, third], axis=0), fold)
        folded = folded[:size] + (folded[size : 2 * size] + folded[2 * size :])
        evens = split(jnp.where(is_even, folded, 0.0))
        odds = split(jnp.where(is_even, 0.0, folded))
        empty = jnp.zeros((size, BLOCK), bf16)
        lefts.append(
            jnp.concatenate(
                [
                    jnp.concatenate([evens[0], evens[0]], axis=1),
                    jnp.concatenate([odds[0], odds[0]], axis=1),
                    jnp.concatenate([evens[1], empty], axis=1),
                    jnp.concatenate([odds[1], empty], axis=1),
                ],
                axis=0,
            )
        )

    sub = iota((8, 128), 0)
    first_block = (lon_me * SEG_BLOCKS * 2 * BLOCK).astype(f32)
    steps = jnp.concatenate(
        [
            (sub * 2 + 1).astype(f32),
            (sub * 16).astype(f32),
            (sub * (2 * BLOCK) + (BLOCK - 1)).astype(f32) + first_block,
        ],
        axis=0,
    )
    steps = jnp.where(iota((24, 128), 0) < 16 + SEG_BLOCKS, steps, 0.0)
    for lat_group in range(4):
        lanes = slice(lat_group * 128, (lat_group + 1) * 128)
        for pair in range(2):
            for g in range(ROWS_DEV):
                n = jnp.full((1, 128), counts[g] * 2, jnp.int32).astype(f32)
                inverse = 1.0 / n
                scale = lax.rsqrt(n * (ROWS_T / 2))
                rights = []
                for u in (pair * 2, pair * 2 + 1):
                    index = u * 4 + lat_group
                    wave = jnp.maximum(wave_ref[index : index + 1, :] - 1.0, 0.0)
                    phase = steps * wave
                    phase = phase - n * jnp.round(phase * inverse)
                    cos_v, sin_v = sincos_quarter(phase * (inverse * (math.pi / 2)))
                    at = (g * 16 + index) * 32
                    turn_s[at : at + 8, :] = cos_v[8:16]
                    turn_s[at + 8 : at + 16, :] = sin_v[8:16]
                    turn_s[at + 16 : at + 24, :] = cos_v[16:] * scale
                    turn_s[at + 24 : at + 32, :] = sin_v[16:] * scale
                    cos_low, sin_low = cos_v[:8], sin_v[:8]
                    cos_h, cos_l, sin_h, sin_l = [], [], [], []
                    for b in range(0, 8, 2):
                        cos_p, sin_p = [], []
                        for r in (b, b + 1):
                            cos_r = turn_s[pl.ds(at + r, 8, stride=0), :]
                            sin_r = turn_s[pl.ds(at + 8 + r, 8, stride=0), :]
                            cos_p.append(cos_low * cos_r - sin_low * sin_r)
                            sin_p.append(sin_low * cos_r + cos_low * sin_r)
                        high, low = split(jnp.concatenate(cos_p, axis=0))
                        cos_h.append(high)
                        cos_l.append(low)
                        high, low = split(jnp.concatenate(sin_p, axis=0))
                        sin_h.append(high)
                        sin_l.append(low)
                    rights.append(jnp.concatenate(cos_h + sin_h + cos_l + sin_l, axis=0))
                both = dot(lefts[g], jnp.concatenate(rights, axis=1))
                both = both[: 2 * size] + both[2 * size :]
                for k in range(2):
                    u = pair * 2 + k
                    at = (g * 16 + u * 4 + lat_group) * 32
                    real = jnp.zeros((8, 128), f32)
                    imag = jnp.zeros((8, 128), f32)
                    for a in range(SEG_BLOCKS):
                        c = both[a * 8 : a * 8 + 8, k * 128 : (k + 1) * 128]
                        s = both[size + a * 8 : size + a * 8 + 8, k * 128 : (k + 1) * 128]
                        cos_a = turn_s[pl.ds(at + 16 + a, 8, stride=0), :]
                        sin_a = turn_s[pl.ds(at + 24 + a, 8, stride=0), :]
                        real = real + (cos_a * c - sin_a * s)
                        imag = imag - (cos_a * s + sin_a * c)
                    row = u * 32 + g * 16
                    spec_s[row : row + 16, lanes] = jnp.concatenate([real, imag], axis=0)
        out_s[lanes, :] = spec_s[:, lanes].T
        copy = pltpu.make_async_copy(out_s.at[lanes, :], out_hbm.at[lanes, :], out_sems.at[lat_group])
        copy.start()
        departures.append(copy)
    for copy in departures:
        copy.wait()


def recur_kernel(wave_ref, row_ref, high_ref, low_ref, poly_s):
    lat_me = lax.axis_index("lat")
    lon_me = lax.axis_index("lon")
    me = lat_me * N_LON + lon_me
    group = me // 32
    lane = iota((1, 128), 1)
    rows = jnp.zeros((1, 128), jnp.int32)
    for part in range(ROWS_DEV):
        for lat in range(N_LAT):
            rows = jnp.where(lane % 32 == part * 16 + lat, row_ref[lat * 2 + part], rows)
    angle = (NLAT_FULL / 2 - 0.5) - rows.astype(f32)
    _, x = sincos_quarter(jnp.broadcast_to(angle * (math.pi / (4 * NLAT_FULL)), (4, 128)))
    log_sin = 0.5 * jnp.log1p(-x * x)

    found = []
    for q in range(4):
        total = jnp.zeros((1, 128), f32)
        for u in range(4):
            mine = wave_ref[pl.ds(u * 4 + group, 1), :]
            value = jnp.sum(
                jnp.where(lane == (me % 32) * 4 + q, mine, 0.0), axis=1, keepdims=True
            )
            total = jnp.where(lane // 32 == u, value, total)
        found.append(total)
    number = jnp.concatenate(found, axis=0)
    m = jnp.maximum(number - 1.0, 0.0)
    limit = jnp.where(number > 0.5, MW - m, 0.0)

    z = m + 1.0
    ratio = (z * (z + 1.0) * (z + 2.0) * (z + 3.0)) / (
        (z + 0.5) * (z + 1.5) * (z + 2.5) * (z + 3.5)
    )
    far = 1.0 / (z + 4.0)
    far2 = far * far
    log_ratio = (
        0.5 * jnp.log(z + 4.0)
        + far * (-1.0 / 8 + far2 * (1.0 / 192 - far2 * (1.0 / 640)))
        + jnp.log(ratio)
    )
    log_start = 0.5 * (
        log_ratio - math.lgamma(1.5) + jnp.where(m > 0.5, math.log(2.0), 0.0)
    )
    start = jnp.exp(log_start + m * log_sin)
    twice = 2.0 * m

    unroll = 16

    def turn(t, state):
        previous, current, shrink = state
        base = (t * unroll).astype(f32)
        for j in range(unroll):
            poly_s[pl.ds(pl.multiple_of(t * (unroll * 4), unroll * 4) + j * 4, 4), :] = current
            step = base + (j + 1.0)
            reach = twice + step
            degree2 = reach + step
            square = degree2 * degree2 - 1.0
            gap = step * reach
            root = lax.rsqrt(square * gap)
            grow = square * root
            previous, current = (
                current,
                (grow * x) * current - (grow * shrink) * previous,
            )
            shrink = gap * root
        return previous, current, shrink

    zero = jnp.zeros((4, 128), f32)
    lax.fori_loop(0, MW // unroll, turn, (zero, start, zero))

    for q in range(4):
        for b in range(MW // 128):
            piece = poly_s[pl.ds(b * 512 + q, 128, stride=4), :]
            within = (iota((128, 128), 0) + b * 128).astype(f32) < limit[q : q + 1]
            piece = jnp.where(within, piece, 0.0).T
            high, low = split(piece)
            high_ref[q * 128 : (q + 1) * 128, b * 128 : (b + 1) * 128] = high
            low_ref[q * 128 : (q + 1) * 128, b * 128 : (b + 1) * 128] = low


def back_kernel(in_ref, high_ref, low_ref, out_ref, sum_s, result_s, sems):
    for lat in range(N_LAT):
        total = in_ref[lat * 32 : lat * 32 + 8, :]
        for part in range(1, 4):
            total = total + in_ref[lat * 32 + part * 8 : lat * 32 + part * 8 + 8, :]
        sum_s[lat * 8 : lat * 8 + 8, :] = total
    lane = iota((16, 128), 1)
    lefts = []
    for pair in range(2):
        rows = []
        for half in range(2):
            q = pair * 2 + half
            x = sum_s[pl.ds(q, 16, stride=8), :] + sum_s[pl.ds(q + 4, 16, stride=8), :]
            for u in range(4):
                for part in range(ROWS_DEV):
                    shift = ((half - part) * 16) % 128
                    moved = x if shift == 0 else pltpu.roll(x, shift, 1)
                    at = u * 32 + half * 16
                    rows.append(jnp.where((lane >= at) & (lane < at + 16), moved, 0.0))
        first = jnp.concatenate(rows[:8], axis=0).T
        second = jnp.concatenate(rows[8:], axis=0).T
        lefts.append(split(jnp.concatenate([first, second], axis=1)))
    copies = []
    for b in range(MW // 256):
        lanes = slice(b * 256, (b + 1) * 256)
        for pair in range(2):
            high, low = lefts[pair]
            rows = slice(pair * 256, (pair + 1) * 256)
            both = dot(jnp.concatenate([high, low], axis=0), high_ref[rows, lanes])
            value = both[:128] + both[128:] + dot(high, low_ref[rows, lanes])
            for s in range(8):
                slot = pair * 8 + s
                if slot < PER_DEV:
                    for part in range(2):
                        at = s * 16 + part * 8
                        result_s[slot, :, part, lanes] = value[at : at + 8]
        copy = pltpu.make_async_copy(
            result_s.at[:, :, :, lanes], out_ref.at[:, :, :, lanes], sems.at[b]
        )
        copy.start()
        copies.append(copy)
    for copy in copies:
        copy.wait()


diffusivity = 1.66
scatter_share = 0.2
heat_gain = 10.0


def shards(
    grid_fields, sun_cosine, surface_albedo, gas_absorb, solar_weight, helper_map, row_lat, wave_owner
):
    vmem = pl.BlockSpec(memory_space=pltpu.VMEM)
    smem = pl.BlockSpec(memory_space=pltpu.SMEM)
    hbm = pl.BlockSpec(memory_space=pl.ANY)
    limits = pltpu.CompilerParams(vmem_limit_bytes=16 * 2**20)
    outgoing, waves = pl.pallas_call(
        front_kernel,
        out_shape=(
            jax.ShapeDtypeStruct((DESTS * 4, 128), f32),
            jax.ShapeDtypeStruct((16, 128), f32),
        ),
        in_specs=[hbm] * 8,
        out_specs=(hbm, hbm),
        scratch_shapes=[
            pltpu.VMEM((ROWS_DEV, K, SEG_BLOCKS * BLOCK), f32),
            pltpu.VMEM((ROWS_DEV, SEG_BLOCKS * BLOCK), f32),
            pltpu.VMEM((ROWS_DEV, SEG_BLOCKS * BLOCK), f32),
            pltpu.VMEM((1, G), f32),
            pltpu.VMEM((1, G), f32),
            pltpu.SMEM((ROWS_DEV, SEG_BLOCKS), jnp.int32),
            pltpu.SMEM((ROWS_T,), jnp.int32),
            pltpu.VMEM((MW // 128, 128), jnp.int32),
            pltpu.VMEM((DESTS * 4, 128), f32),
            pltpu.VMEM((4, 128, 128), bf16),
            pltpu.VMEM((G * 8, 128), bf16),
            pltpu.VMEM((128, 128), f32),
            pltpu.VMEM((ROWS_DEV, SEG_BLOCKS * 8, 128), f32),
            pltpu.VMEM((128, 512), f32),
            pltpu.VMEM((1024, 128), f32),
            pltpu.VMEM((16, 128), f32),
            pltpu.SemaphoreType.DMA((9,)),
            pltpu.SemaphoreType.DMA((5,)),
        ],
        cost_estimate=pl.CostEstimate(flops=2 * 10**8, bytes_accessed=10**6, transcendentals=10**6),
        name="front",
        compiler_params=pltpu.CompilerParams(vmem_limit_bytes=60 * 2**20),
    )(
        grid_fields,
        sun_cosine,
        surface_albedo,
        gas_absorb.reshape(1, G),
        solar_weight.reshape(1, G),
        helper_map,
        row_lat,
        wave_owner.reshape(MW // 128, 128),
    )
    incoming = lax.all_to_all(
        outgoing.reshape(DESTS, 4, 128), ("lat", "lon"), split_axis=0, concat_axis=0, tiled=True
    )
    high, low = pl.pallas_call(
        recur_kernel,
        out_shape=(
            jax.ShapeDtypeStruct((512, MW), bf16),
            jax.ShapeDtypeStruct((512, MW), bf16),
        ),
        in_specs=[vmem, smem],
        out_specs=(vmem, vmem),
        scratch_shapes=[pltpu.VMEM((MW * 4, 128), f32)],
        cost_estimate=pl.CostEstimate(flops=2 * 10**7, bytes_accessed=3 * 10**6, transcendentals=10**6),
        name="recur",
        compiler_params=limits,
    )(waves, row_lat)
    return pl.pallas_call(
        back_kernel,
        out_shape=jax.ShapeDtypeStruct((PER_DEV, K, 2, MW), f32),
        in_specs=[vmem, vmem, vmem],
        out_specs=pl.BlockSpec(memory_space=pl.ANY),
        scratch_shapes=[
            pltpu.VMEM((128, 128), f32),
            pltpu.VMEM((PER_DEV, K, 2, MW), f32),
            pltpu.SemaphoreType.DMA((MW // 256,)),
        ],
        cost_estimate=pl.CostEstimate(flops=5 * 10**8, bytes_accessed=4 * 10**6, transcendentals=0),
        name="back",
        compiler_params=limits,
    )(incoming.reshape(DESTS * 4, 128), high, low)


def solution(mesh):
    placed = (
        P(None, "lat", "lon"),
        P("lat", "lon"),
        P("lat", "lon"),
        P(),
        P(),
        P("lat", "lon"),
        P(),
        P(),
    )
    return jax.shard_map(
        shards,
        mesh=mesh,
        in_specs=placed,
        out_specs=P(("lat", "lon"), None, None, None),
        check_vma=False,
    )
```

```python
import math

import jax
import jax.numpy as jnp
from jax import lax
from jax.experimental import pallas as pl
from jax.experimental.pallas import tpu as pltpu
from jax.sharding import PartitionSpec as P

LEV = 4
BLOCK = 128
NLAT_FULL = 2560
MW = 1280
G = 112
K = 8
SEG_BLOCKS = 6
ROWS_DEV = 2
N_LAT = 16
N_LON = 8
DESTS = N_LAT * N_LON
PER_DEV = 15
MCAP = PER_DEV * N_LON
ROWS_T = N_LAT * ROWS_DEV
LOG2E = math.log2(math.e)

f32 = jnp.float32
bf16 = jnp.bfloat16


def iota(shape, dim):
    return lax.broadcasted_iota(jnp.int32, shape, dim)


def dot(a, b, contract=(1, 0)):
    return lax.dot_general(
        a, b, (((contract[0],), (contract[1],)), ((), ())), preferred_element_type=f32
    )


def split(x):
    high = x.astype(bf16)
    return high, (x - high.astype(f32)).astype(bf16)


def sincos_quarter(r):
    r2 = r * r
    sin_v = r + (r * r2) * (-1.6666654611e-1 + r2 * (8.3321608736e-3 - r2 * 1.9515295891e-4))
    cos_v = 1.0 + r2 * (
        -0.5 + r2 * (4.166664568298827e-2 + r2 * (-1.388731625493765e-3 + r2 * 2.443315711809948e-5))
    )
    for _ in range(2):
        twice = sin_v + sin_v
        cos_v, sin_v = 1.0 - twice * sin_v, twice * cos_v
    return cos_v, sin_v


def slot_of(lane_q, lane_u):
    return (lane_q // 2) * 8 + lane_u * 2 + lane_q % 2


def slot_picks(pick_ref):
    lane = iota((128, 128), 1)
    for u in range(4):
        index = slot_of(lane % 4, u)
        for kind, span in enumerate((N_LON, N_LON // 2)):
            rank = ((lane // 4) % span) * PER_DEV + index
            pick = (iota((128, 128), 0) == rank) & (index < PER_DEV)
            pick_ref[kind * 4 + u] = pick.astype(f32).astype(bf16)


def find_slots(owner_ref, pick_ref, table_ref, order_ref, wave_ref):
    groups = MW // 128
    owner = iota((N_LAT, 128), 0)
    lane = iota((N_LAT, 128), 1)
    hits = [(owner_ref[b : b + 1, :] == owner).astype(f32) for b in range(groups)]
    stacked = jnp.concatenate(hits, axis=0).astype(bf16)
    before = (iota((128, 128), 0) < iota((128, 128), 1)).astype(f32).astype(bf16)
    ahead = dot(stacked, before)
    total = dot(stacked, jnp.ones((128, 128), bf16))
    carry = jnp.zeros((N_LAT, 128), f32)
    table = jnp.zeros((2 * N_LAT, 128), f32)
    for b in range(groups):
        part = slice(b * N_LAT, (b + 1) * N_LAT)
        rank = jnp.sum(hits[b] * (ahead[part] + carry), axis=0, keepdims=True)
        carry = carry + total[part]
        ranked = (rank.astype(jnp.int32) == iota((128, 128), 0)).astype(f32).astype(bf16)
        number = lane + (b * 128 + 1)
        high = ((number >> 4) << 4).astype(f32)
        low = (number & 15).astype(f32)
        both = jnp.concatenate([hits[b] * high, hits[b] * low], axis=0).astype(bf16)
        table = table + dot(both, ranked, (1, 1))
    table_ref[...] = table
    full = carry > (MCAP * 2 / 3)
    below = (iota((N_LAT, N_LAT), 1) < iota((N_LAT, N_LAT), 0)).astype(f32).astype(bf16)
    fulls = dot(below, full.astype(f32).astype(bf16))
    spare = owner.astype(f32) - fulls + N_LAT // 2
    place = jnp.where(full, fulls, spare).astype(jnp.int32)
    order_ref[...] = jnp.sum(jnp.where(place == lane, owner, 0), axis=0, keepdims=True)
    table = table.astype(bf16)
    for u in range(4):
        for kind in range(2):
            found = dot(table, pick_ref[kind * 4 + u])
            found = found[:N_LAT] + found[N_LAT:]
            for g in (0, 1) if kind == 0 else (2,):
                own = place == (g * 4 + lane // 32 if kind == 0 else 8 + lane // 16)
                wave_ref[u * 4 + g : u * 4 + g + 1, :] = jnp.sum(
                    jnp.where(own, found, 0.0), axis=0, keepdims=True
                )


def front_kernel(
    fields_hbm, sun_hbm, ground_hbm, gas_hbm, weight_hbm, lit_hbm, row_hbm, owner_hbm,
    out_hbm, table_hbm,
    fields_ref, sun_ref, ground_ref, gas_ref, weight_ref, lit_ref, row_ref, owner_ref,
    out_s, pick_s, share_s, beam_s, left_s, spec_s, turn_s, wave_ref, table_s, row_s, order_s, turned_s, in_sems, out_sems,
):
    lat_me = lax.axis_index("lat")
    lon_me = lax.axis_index("lon")
    pairs = [
        (owner_hbm, owner_ref),
        (gas_hbm, gas_ref),
        (weight_hbm, weight_ref),
        (row_hbm, row_ref),
        (lit_hbm, lit_ref),
        (sun_hbm, sun_ref),
        (ground_hbm, ground_ref),
    ] + [(fields_hbm.at[:, g, :], fields_ref.at[g]) for g in range(ROWS_DEV)]
    arrivals = [
        pltpu.make_async_copy(source, target, in_sems.at[index])
        for index, (source, target) in enumerate(pairs)
    ]
    for copy in arrivals:
        copy.start()
    slot_picks(pick_s)
    out_s[...] = jnp.zeros_like(out_s)
    arrivals[0].wait()
    for copy in arrivals[1:]:
        copy.wait()
    find_slots(owner_ref, pick_s, table_s, row_s, wave_ref)

    def column(row):
        padded = jnp.concatenate([row, jnp.ones((1, 128 - G), f32)], axis=1)
        return jnp.broadcast_to(padded, (128, 128)).T

    def thirds(x):
        first = x.astype(bf16).astype(f32)
        second = (x - first).astype(bf16).astype(f32)
        return first, second, (x - first - second).astype(bf16).astype(f32)

    kinds = 2 * LEV
    total_weight = jnp.sum(weight_ref[...], axis=1, keepdims=True)
    gas = column(gas_ref[...])
    share = column(weight_ref[...] * (heat_gain / total_weight))
    beam_s[...] = share
    gas_1, gas_2, gas_3 = thirds(gas)
    log_1, log_2, log_3 = thirds(jnp.log2(share))
    lane = iota((8, 128), 1)
    term = lane // kinds
    for part in range(G // 8):
        rows = slice(part * 8, (part + 1) * 8)
        factor = jnp.where(
            (term == 1) | (term == 4), gas_2[rows], jnp.where(term == 2, gas_3[rows], gas_1[rows])
        )
        tail = jnp.where(
            lane < 6 * kinds + 3,
            1.0,
            jnp.where(
                lane == 6 * kinds + 3,
                log_1[rows],
                jnp.where(lane == 6 * kinds + 4, log_2[rows], log_3[rows]),
            ),
        )
        tail = jnp.where((term == 6) & (lane < 6 * kinds + 6), tail, 0.0)
        pieces = []
        for kind in range(kinds):
            own = jnp.where((lane % kinds == kind) & (term < 6), factor, 0.0)
            pieces.append(jnp.where(term == 6, tail, own) if kind < LEV else own)
        share_s[part * 64 : (part + 1) * 64, :] = jnp.concatenate(pieces, axis=0).astype(bf16)

    counts = []
    for g in range(ROWS_DEV):
        row = row_ref[lat_me * ROWS_DEV + g]
        counts.append(20 + 4 * jnp.minimum(row, NLAT_FULL - 1 - row))

    sub = iota((8, BLOCK), 0)
    tile = lambda row: jnp.broadcast_to(row, (8, BLOCK))
    for a in range(SEG_BLOCKS):
        columns = slice(a * BLOCK, (a + 1) * BLOCK)
        paths, grounds, suns = [], [], []
        for g in range(ROWS_DEV):
            x = fields_ref[g, :, columns]
            depth = jnp.maximum(x, 0.0) + jnp.log1p(jnp.exp(-jnp.abs(x)))
            sun = sun_ref[g : g + 1, columns]
            suns.append(sun)
            grounds.append(ground_ref[g : g + 1, columns])
            slant = tile(depth[:1])
            for level in range(1, LEV):
                slant = slant + jnp.where(sub >= level, tile(depth[level : level + 1]), 0.0)
            path = jnp.where(
                sub < LEV,
                slant * (-LOG2E / sun),
                pltpu.roll(depth, LEV, 0) * (-LOG2E * diffusivity),
            )
            path_1, path_2, path_3 = thirds(path)
            logs = thirds(tile(jnp.log2(sun * scatter_share)))
            tail = jnp.where(
                sub == 0, logs[0], jnp.where(sub == 1, logs[1], jnp.where(sub == 2, logs[2], 1.0))
            )
            zero = jnp.zeros((8, BLOCK), f32)
            stack = [path_1, path_1, path_1, path_2, path_2, path_3, tail] + [zero] * 9
            paths.append(jnp.concatenate(stack, axis=0).astype(bf16))
        right = jnp.concatenate(paths, axis=1)
        nets = [[jnp.zeros((8, BLOCK), f32) for _ in range(LEV + 1)] for _ in range(ROWS_DEV)]
        beams = [[jnp.zeros((8, BLOCK), f32) for _ in range(LEV + 1)] for _ in range(ROWS_DEV)]
        for g in range(ROWS_DEV):
            beams[g][0] = tile(suns[g] * (scatter_share * heat_gain / 8))
        ground_b = [tile(ground) for ground in grounds]
        sun_b = [tile(sun * scatter_share) for sun in suns]
        for part in range(G // 8):
            passing = jnp.exp2(dot(share_s[part * 64 : (part + 1) * 64, :], right))
            for g in range(ROWS_DEV):
                net, beam_sum = nets[g], beams[g]
                pick = lambda kind: passing[kind * 8 : kind * 8 + 8, g * BLOCK : (g + 1) * BLOCK]
                beam = sun_b[g] * beam_s[part * 8 : (part + 1) * 8, :]
                down, downs, sources = None, [], []
                for level in range(LEV):
                    after = pick(level)
                    source = beam - after
                    beam = after
                    down = source if down is None else down * pick(LEV + level) + source
                    beam_sum[level + 1] = beam_sum[level + 1] + beam
                    downs.append(down)
                    sources.append(source)
                net[LEV] = net[LEV] + down
                upward = ground_b[g] * (beam * (1.0 / scatter_share) + down)
                for level in range(LEV - 1, -1, -1):
                    upward = upward * pick(LEV + level) + sources[level]
                    if level:
                        net[level] = net[level] + (downs[level - 1] - upward)
                    else:
                        net[level] = net[level] - upward
        for g in range(ROWS_DEV):
            levels = [
                net + beam_sum * (1.0 / scatter_share) for net, beam_sum in zip(nets[g], beams[g])
            ]
            levels[LEV] = levels[LEV] * (1.0 - grounds[g])
            is_lit = lit_ref[g, a] >= 0
            heated = fields_ref[g, :, columns]
            for level in range(LEV):
                heat = jnp.sum(levels[level] - levels[level + 1], axis=0, keepdims=True)
                heat = jnp.where(is_lit, heat, 0.0)
                heated = heated + jnp.where(sub == LEV + level, heat, 0.0)
            first = (lon_me * SEG_BLOCKS + a) * BLOCK
            heated = jnp.where(iota((8, BLOCK), 1) + first < counts[g], heated, 0.0)
            left_s[g, a * 8 : (a + 1) * 8, :] = heated

    offset, place = iota((BLOCK, BLOCK), 0), iota((BLOCK, BLOCK), 1)
    half = BLOCK // 2
    step = place % half
    fold = jnp.where(offset == half + step, 1.0, 0.0)
    mirror = jnp.where(offset == half - 1 - step, 1.0, 0.0)
    fold = (fold + jnp.where(place < half, mirror, -mirror)).astype(bf16)
    size = SEG_BLOCKS * 8
    is_even = iota((size, BLOCK), 1) < half
    lefts = []
    for g in range(ROWS_DEV):
        x = left_s[g]
        first = x.astype(bf16)
        second, third = split(x - first.astype(f32))
        folded = dot(jnp.concatenate([first, second, third], axis=0), fold)
        folded = folded[:size] + (folded[size : 2 * size] + folded[2 * size :])
        evens = split(jnp.where(is_even, folded, 0.0))
        odds = split(jnp.where(is_even, 0.0, folded))
        empty = jnp.zeros((size, BLOCK), bf16)
        lefts.append(
            jnp.concatenate(
                [
                    jnp.concatenate([evens[0], evens[0]], axis=1),
                    jnp.concatenate([odds[0], odds[0]], axis=1),
                    jnp.concatenate([evens[1], empty], axis=1),
                    jnp.concatenate([odds[1], empty], axis=1),
                ],
                axis=0,
            )
        )

    sub = iota((8, 128), 0)
    first_block = (lon_me * SEG_BLOCKS * 2 * BLOCK).astype(f32)
    steps = jnp.concatenate(
        [
            (sub * 2 + 1).astype(f32),
            (sub * 16).astype(f32),
            (sub * (2 * BLOCK) + (BLOCK - 1)).astype(f32) + first_block,
        ],
        axis=0,
    )
    steps = jnp.where(iota((24, 128), 0) < 16 + SEG_BLOCKS, steps, 0.0)
    for lat_group in range(3):
        lanes = slice(lat_group * 128, (lat_group + 1) * 128)
        for pair in range(2):
            for g in range(ROWS_DEV):
                n = jnp.full((1, 128), counts[g] * 2, jnp.int32).astype(f32)
                inverse = 1.0 / n
                scale = lax.rsqrt(n * (ROWS_T / 2))
                rights = []
                for u in (pair * 2, pair * 2 + 1):
                    index = u * 4 + lat_group
                    wave = jnp.maximum(wave_ref[index : index + 1, :] - 1.0, 0.0)
                    phase = steps * wave
                    phase = phase - n * jnp.round(phase * inverse)
                    cos_v, sin_v = sincos_quarter(phase * (inverse * (math.pi / 2)))
                    at = (g * 16 + index) * 32
                    turn_s[at : at + 8, :] = cos_v[8:16]
                    turn_s[at + 8 : at + 16, :] = sin_v[8:16]
                    turn_s[at + 16 : at + 24, :] = cos_v[16:] * scale
                    turn_s[at + 24 : at + 32, :] = sin_v[16:] * scale
                    cos_low, sin_low = cos_v[:8], sin_v[:8]
                    cos_h, cos_l, sin_h, sin_l = [], [], [], []
                    for b in range(0, 8, 2):
                        cos_p, sin_p = [], []
                        for r in (b, b + 1):
                            cos_r = turn_s[pl.ds(at + r, 8, stride=0), :]
                            sin_r = turn_s[pl.ds(at + 8 + r, 8, stride=0), :]
                            cos_p.append(cos_low * cos_r - sin_low * sin_r)
                            sin_p.append(sin_low * cos_r + cos_low * sin_r)
                        high, low = split(jnp.concatenate(cos_p, axis=0))
                        cos_h.append(high)
                        cos_l.append(low)
                        high, low = split(jnp.concatenate(sin_p, axis=0))
                        sin_h.append(high)
                        sin_l.append(low)
                    rights.append(jnp.concatenate(cos_h + sin_h + cos_l + sin_l, axis=0))
                both = dot(lefts[g], jnp.concatenate(rights, axis=1))
                both = both[: 2 * size] + both[2 * size :]
                for k in range(2):
                    u = pair * 2 + k
                    at = (g * 16 + u * 4 + lat_group) * 32
                    real = jnp.zeros((8, 128), f32)
                    imag = jnp.zeros((8, 128), f32)
                    for a in range(SEG_BLOCKS):
                        c = both[a * 8 : a * 8 + 8, k * 128 : (k + 1) * 128]
                        s = both[size + a * 8 : size + a * 8 + 8, k * 128 : (k + 1) * 128]
                        cos_a = turn_s[pl.ds(at + 16 + a, 8, stride=0), :]
                        sin_a = turn_s[pl.ds(at + 24 + a, 8, stride=0), :]
                        real = real + (cos_a * c - sin_a * s)
                        imag = imag - (cos_a * s + sin_a * c)
                    row = u * 32 + g * 16
                    spec_s[row : row + 16, lanes] = jnp.concatenate([real, imag], axis=0)
        turned_s[lanes, :] = spec_s[:, lanes].T
        if lat_group == 0:
            ordering = pltpu.make_async_copy(row_s, order_s, in_sems.at[9])
            leaving = pltpu.make_async_copy(table_s, table_hbm, out_sems.at[0])
            ordering.start()
            leaving.start()
    ordering.wait()
    for place in range(N_LAT):
        span = 32 if place < 8 else 16
        first = place * 32 if place < 8 else 256 + (place - 8) * 16
        start = pl.multiple_of(order_s[0, place] * 32, 32)
        out_s[pl.ds(start, span), :] = turned_s[first : first + span, :]
    sending = pltpu.make_async_copy(out_s, out_hbm, out_sems.at[1])
    sending.start()
    leaving.wait()
    sending.wait()


def recur_kernel(table_ref, row_ref, high_ref, low_ref, poly_s):
    lat_me = lax.axis_index("lat")
    lon_me = lax.axis_index("lon")
    lane = iota((1, 128), 1)
    rows = jnp.zeros((1, 128), jnp.int32)
    for part in range(ROWS_DEV):
        for lat in range(N_LAT):
            rows = jnp.where(lane % 32 == part * 16 + lat, row_ref[lat * 2 + part], rows)
    angle = (NLAT_FULL / 2 - 0.5) - rows.astype(f32)
    _, x = sincos_quarter(jnp.broadcast_to(angle * (math.pi / (4 * NLAT_FULL)), (4, 128)))
    log_sin = 0.5 * jnp.log1p(-x * x)

    table = table_ref[...].astype(bf16)
    found = []
    for q in range(4):
        index = slot_of(q, iota((128, 128), 1) // 32)
        pick = (iota((128, 128), 0) == lon_me * PER_DEV + index) & (index < PER_DEV)
        both = dot(table, pick.astype(f32).astype(bf16))
        mine = jnp.where(iota((N_LAT, 128), 0) == lat_me, both[:N_LAT] + both[N_LAT:], 0.0)
        found.append(jnp.sum(mine, axis=0, keepdims=True))
    number = jnp.concatenate(found, axis=0)
    m = jnp.maximum(number - 1.0, 0.0)
    limit = jnp.where(number > 0.5, MW - m, 0.0)

    z = m + 1.0
    ratio = (z * (z + 1.0) * (z + 2.0) * (z + 3.0)) / (
        (z + 0.5) * (z + 1.5) * (z + 2.5) * (z + 3.5)
    )
    far = 1.0 / (z + 4.0)
    far2 = far * far
    log_ratio = (
        0.5 * jnp.log(z + 4.0)
        + far * (-1.0 / 8 + far2 * (1.0 / 192 - far2 * (1.0 / 640)))
        + jnp.log(ratio)
    )
    log_start = 0.5 * (
        log_ratio - math.lgamma(1.5) + jnp.where(m > 0.5, math.log(2.0), 0.0)
    )
    start = jnp.exp(log_start + m * log_sin)
    twice = 2.0 * m

    unroll = 16

    def turn(t, state):
        previous, current, shrink = state
        base = (t * unroll).astype(f32)
        for j in range(unroll):
            poly_s[pl.ds(pl.multiple_of(t * (unroll * 4), unroll * 4) + j * 4, 4), :] = current
            step = base + (j + 1.0)
            reach = twice + step
            degree2 = reach + step
            square = degree2 * degree2 - 1.0
            gap = step * reach
            root = lax.rsqrt(square * gap)
            grow = square * root
            previous, current = (
                current,
                (grow * x) * current - (grow * shrink) * previous,
            )
            shrink = gap * root
        return previous, current, shrink

    zero = jnp.zeros((4, 128), f32)
    lax.fori_loop(0, MW // unroll, turn, (zero, start, zero))

    for q in range(4):
        for b in range(MW // 128):
            piece = poly_s[pl.ds(b * 512 + q, 128, stride=4), :]
            within = (iota((128, 128), 0) + b * 128).astype(f32) < limit[q : q + 1]
            piece = jnp.where(within, piece, 0.0).T
            high, low = split(piece)
            high_ref[q * 128 : (q + 1) * 128, b * 128 : (b + 1) * 128] = high
            low_ref[q * 128 : (q + 1) * 128, b * 128 : (b + 1) * 128] = low


def back_kernel(in_ref, high_ref, low_ref, out_ref, sum_s, result_s, sems):
    for lat in range(N_LAT):
        total = in_ref[lat * 32 : lat * 32 + 8, :]
        for part in range(1, 4):
            total = total + in_ref[lat * 32 + part * 8 : lat * 32 + part * 8 + 8, :]
        sum_s[lat * 8 : lat * 8 + 8, :] = total
    lane = iota((16, 128), 1)
    lefts = []
    for pair in range(2):
        rows = []
        for half in range(2):
            q = pair * 2 + half
            x = sum_s[pl.ds(q, 16, stride=8), :] + sum_s[pl.ds(q + 4, 16, stride=8), :]
            for u in range(4):
                for part in range(ROWS_DEV):
                    shift = ((half - part) * 16) % 128
                    moved = x if shift == 0 else pltpu.roll(x, shift, 1)
                    at = u * 32 + half * 16
                    rows.append(jnp.where((lane >= at) & (lane < at + 16), moved, 0.0))
        first = jnp.concatenate(rows[:8], axis=0).T
        second = jnp.concatenate(rows[8:], axis=0).T
        lefts.append(split(jnp.concatenate([first, second], axis=1)))
    copies = []
    for b in range(MW // 256):
        lanes = slice(b * 256, (b + 1) * 256)
        for pair in range(2):
            high, low = lefts[pair]
            rows = slice(pair * 256, (pair + 1) * 256)
            both = dot(jnp.concatenate([high, low], axis=0), high_ref[rows, lanes])
            value = both[:128] + both[128:] + dot(high, low_ref[rows, lanes])
            for s in range(8):
                slot = pair * 8 + s
                if slot < PER_DEV:
                    for part in range(2):
                        at = s * 16 + part * 8
                        result_s[slot, :, part, lanes] = value[at : at + 8]
        copy = pltpu.make_async_copy(
            result_s.at[:, :, :, lanes], out_ref.at[:, :, :, lanes], sems.at[b]
        )
        copy.start()
        copies.append(copy)
    for copy in copies:
        copy.wait()


diffusivity = 1.66
scatter_share = 0.2
heat_gain = 10.0


def shards(
    grid_fields, sun_cosine, surface_albedo, gas_absorb, solar_weight, helper_map, row_lat, wave_owner
):
    vmem = pl.BlockSpec(memory_space=pltpu.VMEM)
    smem = pl.BlockSpec(memory_space=pltpu.SMEM)
    hbm = pl.BlockSpec(memory_space=pl.ANY)
    limits = pltpu.CompilerParams(vmem_limit_bytes=16 * 2**20)
    outgoing, table = pl.pallas_call(
        front_kernel,
        out_shape=(
            jax.ShapeDtypeStruct((DESTS * 4, 128), f32),
            jax.ShapeDtypeStruct((2 * N_LAT, 128), f32),
        ),
        in_specs=[hbm] * 8,
        out_specs=(hbm, hbm),
        scratch_shapes=[
            pltpu.VMEM((ROWS_DEV, K, SEG_BLOCKS * BLOCK), f32),
            pltpu.VMEM((ROWS_DEV, SEG_BLOCKS * BLOCK), f32),
            pltpu.VMEM((ROWS_DEV, SEG_BLOCKS * BLOCK), f32),
            pltpu.VMEM((1, G), f32),
            pltpu.VMEM((1, G), f32),
            pltpu.SMEM((ROWS_DEV, SEG_BLOCKS), jnp.int32),
            pltpu.SMEM((ROWS_T,), jnp.int32),
            pltpu.VMEM((MW // 128, 128), jnp.int32),
            pltpu.VMEM((DESTS * 4, 128), f32),
            pltpu.VMEM((8, 128, 128), bf16),
            pltpu.VMEM((G * 8, 128), bf16),
            pltpu.VMEM((128, 128), f32),
            pltpu.VMEM((ROWS_DEV, SEG_BLOCKS * 8, 128), f32),
            pltpu.VMEM((128, 384), f32),
            pltpu.VMEM((1024, 128), f32),
            pltpu.VMEM((16, 128), f32),
            pltpu.VMEM((2 * N_LAT, 128), f32),
            pltpu.VMEM((1, 128), jnp.int32),
            pltpu.SMEM((1, 128), jnp.int32),
            pltpu.VMEM((DESTS * 3, 128), f32),
            pltpu.SemaphoreType.DMA((10,)),
            pltpu.SemaphoreType.DMA((2,)),
        ],
        cost_estimate=pl.CostEstimate(flops=2 * 10**8, bytes_accessed=10**6, transcendentals=10**6),
        name="front",
        compiler_params=pltpu.CompilerParams(vmem_limit_bytes=60 * 2**20),
    )(
        grid_fields,
        sun_cosine,
        surface_albedo,
        gas_absorb.reshape(1, G),
        solar_weight.reshape(1, G),
        helper_map,
        row_lat,
        wave_owner.reshape(MW // 128, 128),
    )
    incoming = lax.all_to_all(
        outgoing.reshape(DESTS, 4, 128), ("lat", "lon"), split_axis=0, concat_axis=0, tiled=True
    )
    high, low = pl.pallas_call(
        recur_kernel,
        out_shape=(
            jax.ShapeDtypeStruct((512, MW), bf16),
            jax.ShapeDtypeStruct((512, MW), bf16),
        ),
        in_specs=[vmem, smem],
        out_specs=(vmem, vmem),
        scratch_shapes=[pltpu.VMEM((MW * 4, 128), f32)],
        cost_estimate=pl.CostEstimate(flops=2 * 10**7, bytes_accessed=3 * 10**6, transcendentals=10**6),
        name="recur",
        compiler_params=limits,
    )(table, row_lat)
    return pl.pallas_call(
        back_kernel,
        out_shape=jax.ShapeDtypeStruct((PER_DEV, K, 2, MW), f32),
        in_specs=[vmem, vmem, vmem],
        out_specs=pl.BlockSpec(memory_space=pl.ANY),
        scratch_shapes=[
            pltpu.VMEM((128, 128), f32),
            pltpu.VMEM((PER_DEV, K, 2, MW), f32),
            pltpu.SemaphoreType.DMA((MW // 256,)),
        ],
        cost_estimate=pl.CostEstimate(flops=5 * 10**8, bytes_accessed=4 * 10**6, transcendentals=0),
        name="back",
        compiler_params=limits,
    )(incoming.reshape(DESTS * 4, 128), high, low)


def solution(mesh):
    placed = (
        P(None, "lat", "lon"),
        P("lat", "lon"),
        P("lat", "lon"),
        P(),
        P(),
        P("lat", "lon"),
        P(),
        P(),
    )
    return jax.shard_map(
        shards,
        mesh=mesh,
        in_specs=placed,
        out_specs=P(("lat", "lon"), None, None, None),
        check_vma=False,
    )
```

```python
import math

import jax
import jax.numpy as jnp
from jax import lax
from jax.experimental import pallas as pl
from jax.experimental.pallas import tpu as pltpu
from jax.sharding import PartitionSpec as P

LEV = 4
BLOCK = 128
NLAT_FULL = 2560
MW = 1280
G = 112
K = 8
SEG_BLOCKS = 6
ROWS_DEV = 2
N_LAT = 16
N_LON = 8
DESTS = N_LAT * N_LON
PER_DEV = 15
MCAP = PER_DEV * N_LON
ROWS_T = N_LAT * ROWS_DEV
LOG2E = math.log2(math.e)

f32 = jnp.float32
bf16 = jnp.bfloat16


def iota(shape, dim):
    return lax.broadcasted_iota(jnp.int32, shape, dim)


def dot(a, b, contract=(1, 0)):
    return lax.dot_general(
        a, b, (((contract[0],), (contract[1],)), ((), ())), preferred_element_type=f32
    )


def split(x):
    high = x.astype(bf16)
    return high, (x - high.astype(f32)).astype(bf16)


def sincos_quarter(r):
    r2 = r * r
    sin_v = r + (r * r2) * (-1.6666654611e-1 + r2 * (8.3321608736e-3 - r2 * 1.9515295891e-4))
    cos_v = 1.0 + r2 * (
        -0.5 + r2 * (4.166664568298827e-2 + r2 * (-1.388731625493765e-3 + r2 * 2.443315711809948e-5))
    )
    for _ in range(2):
        twice = sin_v + sin_v
        cos_v, sin_v = 1.0 - twice * sin_v, twice * cos_v
    return cos_v, sin_v


def slot_of(lane_q, lane_u):
    return (lane_q // 2) * 8 + lane_u * 2 + lane_q % 2


def slot_picks(pick_ref):
    lane = iota((128, 128), 1)
    for u in range(4):
        index = slot_of(lane % 4, u)
        for kind, span in enumerate((N_LON, N_LON // 2)):
            rank = ((lane // 4) % span) * PER_DEV + index
            pick = (iota((128, 128), 0) == rank) & (index < PER_DEV)
            pick_ref[kind * 4 + u] = pick.astype(f32).astype(bf16)


def find_slots(owner_ref, pick_ref, table_ref, order_ref, wave_ref):
    groups = MW // 128
    owner = iota((N_LAT, 128), 0)
    lane = iota((N_LAT, 128), 1)
    hits = [(owner_ref[b : b + 1, :] == owner).astype(f32) for b in range(groups)]
    stacked = jnp.concatenate(hits, axis=0).astype(bf16)
    before = (iota((128, 128), 0) < iota((128, 128), 1)).astype(f32).astype(bf16)
    ahead = dot(stacked, before)
    total = dot(stacked, jnp.ones((128, 128), bf16))
    carry = jnp.zeros((N_LAT, 128), f32)
    table = jnp.zeros((2 * N_LAT, 128), f32)
    for b in range(groups):
        part = slice(b * N_LAT, (b + 1) * N_LAT)
        rank = jnp.sum(hits[b] * (ahead[part] + carry), axis=0, keepdims=True)
        carry = carry + total[part]
        ranked = (rank.astype(jnp.int32) == iota((128, 128), 0)).astype(f32).astype(bf16)
        number = lane + (b * 128 + 1)
        high = ((number >> 4) << 4).astype(f32)
        low = (number & 15).astype(f32)
        both = jnp.concatenate([hits[b] * high, hits[b] * low], axis=0).astype(bf16)
        table = table + dot(both, ranked, (1, 1))
    table_ref[...] = table
    full = carry > (MCAP * 2 / 3)
    below = (iota((N_LAT, N_LAT), 1) < iota((N_LAT, N_LAT), 0)).astype(f32).astype(bf16)
    fulls = dot(below, full.astype(f32).astype(bf16))
    spare = owner.astype(f32) - fulls + N_LAT // 2
    place = jnp.where(full, fulls, spare).astype(jnp.int32)
    order_ref[...] = jnp.sum(jnp.where(place == lane, owner, 0), axis=0, keepdims=True)
    table = table.astype(bf16)
    for u in range(4):
        for kind in range(2):
            found = dot(table, pick_ref[kind * 4 + u])
            found = found[:N_LAT] + found[N_LAT:]
            for g in (0, 1) if kind == 0 else (2,):
                own = place == (g * 4 + lane // 32 if kind == 0 else 8 + lane // 16)
                wave_ref[u * 4 + g : u * 4 + g + 1, :] = jnp.sum(
                    jnp.where(own, found, 0.0), axis=0, keepdims=True
                )


def front_kernel(
    fields_hbm, sun_hbm, ground_hbm, gas_hbm, weight_hbm, lit_hbm, row_hbm, owner_hbm,
    out_hbm, table_hbm,
    fields_ref, sun_ref, ground_ref, gas_ref, weight_ref, lit_ref, row_ref, owner_ref,
    out_s, pick_s, share_s, beam_s, left_s, spec_s, turn_s, wave_ref, table_s, row_s, order_s, turned_s, in_sems, out_sems,
):
    lat_me = lax.axis_index("lat")
    lon_me = lax.axis_index("lon")
    pairs = [
        (owner_hbm, owner_ref),
        (gas_hbm, gas_ref),
        (weight_hbm, weight_ref),
        (row_hbm, row_ref),
        (lit_hbm, lit_ref),
        (sun_hbm, sun_ref),
        (ground_hbm, ground_ref),
    ] + [(fields_hbm.at[:, g, :], fields_ref.at[g]) for g in range(ROWS_DEV)]
    arrivals = [
        pltpu.make_async_copy(source, target, in_sems.at[index])
        for index, (source, target) in enumerate(pairs)
    ]
    for copy in arrivals:
        copy.start()
    slot_picks(pick_s)
    out_s[...] = jnp.zeros_like(out_s)
    arrivals[0].wait()
    for copy in arrivals[1:]:
        copy.wait()
    find_slots(owner_ref, pick_s, table_s, row_s, wave_ref)

    def column(row):
        padded = jnp.concatenate([row, jnp.ones((1, 128 - G), f32)], axis=1)
        return jnp.broadcast_to(padded, (128, 128)).T

    def thirds(x):
        first = x.astype(bf16).astype(f32)
        second = (x - first).astype(bf16).astype(f32)
        return first, second, (x - first - second).astype(bf16).astype(f32)

    kinds = 2 * LEV
    total_weight = jnp.sum(weight_ref[...], axis=1, keepdims=True)
    gas = column(gas_ref[...])
    share = column(weight_ref[...] * (heat_gain / total_weight))
    beam_s[...] = share
    gas_1, gas_2, gas_3 = thirds(gas)
    log_1, log_2, log_3 = thirds(jnp.log2(share))
    lane = iota((8, 128), 1)
    term = lane // kinds
    for part in range(G // 8):
        rows = slice(part * 8, (part + 1) * 8)
        factor = jnp.where(
            (term == 1) | (term == 4), gas_2[rows], jnp.where(term == 2, gas_3[rows], gas_1[rows])
        )
        tail = jnp.where(
            lane < 6 * kinds + 3,
            1.0,
            jnp.where(
                lane == 6 * kinds + 3,
                log_1[rows],
                jnp.where(lane == 6 * kinds + 4, log_2[rows], log_3[rows]),
            ),
        )
        tail = jnp.where((term == 6) & (lane < 6 * kinds + 6), tail, 0.0)
        pieces = []
        for kind in range(kinds):
            own = jnp.where((lane % kinds == kind) & (term < 6), factor, 0.0)
            pieces.append(jnp.where(term == 6, tail, own) if kind < LEV else own)
        share_s[part * 64 : (part + 1) * 64, :] = jnp.concatenate(pieces, axis=0).astype(bf16)

    counts = []
    for g in range(ROWS_DEV):
        row = row_ref[lat_me * ROWS_DEV + g]
        counts.append(20 + 4 * jnp.minimum(row, NLAT_FULL - 1 - row))

    sub = iota((8, BLOCK), 0)
    tile = lambda row: jnp.broadcast_to(row, (8, BLOCK))
    for a in range(SEG_BLOCKS):
        columns = slice(a * BLOCK, (a + 1) * BLOCK)
        paths, grounds, suns = [], [], []
        for g in range(ROWS_DEV):
            x = fields_ref[g, :, columns]
            depth = jnp.maximum(x, 0.0) + jnp.log1p(jnp.exp(-jnp.abs(x)))
            sun = sun_ref[g : g + 1, columns]
            suns.append(sun)
            grounds.append(ground_ref[g : g + 1, columns])
            slant = tile(depth[:1])
            for level in range(1, LEV):
                slant = slant + jnp.where(sub >= level, tile(depth[level : level + 1]), 0.0)
            path = jnp.where(
                sub < LEV,
                slant * (-LOG2E / sun),
                pltpu.roll(depth, LEV, 0) * (-LOG2E * diffusivity),
            )
            path_1, path_2, path_3 = thirds(path)
            logs = thirds(tile(jnp.log2(sun * scatter_share)))
            tail = jnp.where(
                sub == 0, logs[0], jnp.where(sub == 1, logs[1], jnp.where(sub == 2, logs[2], 1.0))
            )
            zero = jnp.zeros((8, BLOCK), f32)
            stack = [path_1, path_1, path_1, path_2, path_2, path_3, tail] + [zero] * 9
            paths.append(jnp.concatenate(stack, axis=0).astype(bf16))
        right = jnp.concatenate(paths, axis=1)
        nets = [[jnp.zeros((8, BLOCK), f32) for _ in range(LEV + 1)] for _ in range(ROWS_DEV)]
        beams = [[jnp.zeros((8, BLOCK), f32) for _ in range(LEV + 1)] for _ in range(ROWS_DEV)]
        for g in range(ROWS_DEV):
            beams[g][0] = tile(suns[g] * (scatter_share * heat_gain / 8))
        ground_b = [tile(ground) for ground in grounds]
        sun_b = [tile(sun * scatter_share) for sun in suns]
        for g in range(ROWS_DEV):
            for part in range(G // 8):
                passing = jnp.exp2(dot(share_s[part * 64 : (part + 1) * 64, :], paths[g]))
                net, beam_sum = nets[g], beams[g]
                pick = lambda kind: passing[kind * 8 : kind * 8 + 8]
                beam = sun_b[g] * beam_s[part * 8 : (part + 1) * 8, :]
                down, downs, sources = None, [], []
                for level in range(LEV):
                    after = pick(level)
                    source = beam - after
                    beam = after
                    down = source if down is None else down * pick(LEV + level) + source
                    beam_sum[level + 1] = beam_sum[level + 1] + beam
                    downs.append(down)
                    sources.append(source)
                net[LEV] = net[LEV] + down
                upward = ground_b[g] * (beam * (1.0 / scatter_share) + down)
                for level in range(LEV - 1, -1, -1):
                    upward = upward * pick(LEV + level) + sources[level]
                    if level:
                        net[level] = net[level] + (downs[level - 1] - upward)
                    else:
                        net[level] = net[level] - upward
        for g in range(ROWS_DEV):
            levels = [
                net + beam_sum * (1.0 / scatter_share) for net, beam_sum in zip(nets[g], beams[g])
            ]
            levels[LEV] = levels[LEV] * (1.0 - grounds[g])
            is_lit = lit_ref[g, a] >= 0
            heated = fields_ref[g, :, columns]
            for level in range(LEV):
                heat = jnp.sum(levels[level] - levels[level + 1], axis=0, keepdims=True)
                heat = jnp.where(is_lit, heat, 0.0)
                heated = heated + jnp.where(sub == LEV + level, heat, 0.0)
            first = (lon_me * SEG_BLOCKS + a) * BLOCK
            heated = jnp.where(iota((8, BLOCK), 1) + first < counts[g], heated, 0.0)
            left_s[g, a * 8 : (a + 1) * 8, :] = heated

    offset, place = iota((BLOCK, BLOCK), 0), iota((BLOCK, BLOCK), 1)
    half = BLOCK // 2
    step = place % half
    fold = jnp.where(offset == half + step, 1.0, 0.0)
    mirror = jnp.where(offset == half - 1 - step, 1.0, 0.0)
    fold = (fold + jnp.where(place < half, mirror, -mirror)).astype(bf16)
    size = SEG_BLOCKS * 8
    is_even = iota((size, BLOCK), 1) < half
    lefts = []
    for g in range(ROWS_DEV):
        x = left_s[g]
        first = x.astype(bf16)
        second, third = split(x - first.astype(f32))
        folded = dot(jnp.concatenate([first, second, third], axis=0), fold)
        folded = folded[:size] + (folded[size : 2 * size] + folded[2 * size :])
        evens = split(jnp.where(is_even, folded, 0.0))
        odds = split(jnp.where(is_even, 0.0, folded))
        empty = jnp.zeros((size, BLOCK), bf16)
        lefts.append(
            jnp.concatenate(
                [
                    jnp.concatenate([evens[0], evens[0]], axis=1),
                    jnp.concatenate([odds[0], odds[0]], axis=1),
                    jnp.concatenate([evens[1], empty], axis=1),
                    jnp.concatenate([odds[1], empty], axis=1),
                ],
                axis=0,
            )
        )

    sub = iota((8, 128), 0)
    first_block = (lon_me * SEG_BLOCKS * 2 * BLOCK).astype(f32)
    steps = jnp.concatenate(
        [
            (sub * 2 + 1).astype(f32),
            (sub * 16).astype(f32),
            (sub * (2 * BLOCK) + (BLOCK - 1)).astype(f32) + first_block,
        ],
        axis=0,
    )
    steps = jnp.where(iota((24, 128), 0) < 16 + SEG_BLOCKS, steps, 0.0)
    for lat_group in range(3):
        lanes = slice(lat_group * 128, (lat_group + 1) * 128)
        for pair in range(2):
            for g in range(ROWS_DEV):
                n = jnp.full((1, 128), counts[g] * 2, jnp.int32).astype(f32)
                inverse = 1.0 / n
                scale = lax.rsqrt(n * (ROWS_T / 2))
                rights = []
                for u in (pair * 2, pair * 2 + 1):
                    index = u * 4 + lat_group
                    wave = jnp.maximum(wave_ref[index : index + 1, :] - 1.0, 0.0)
                    phase = steps * wave
                    phase = phase - n * jnp.round(phase * inverse)
                    cos_v, sin_v = sincos_quarter(phase * (inverse * (math.pi / 2)))
                    at = (g * 16 + index) * 32
                    turn_s[at : at + 8, :] = cos_v[8:16]
                    turn_s[at + 8 : at + 16, :] = sin_v[8:16]
                    turn_s[at + 16 : at + 24, :] = cos_v[16:] * scale
                    turn_s[at + 24 : at + 32, :] = sin_v[16:] * scale
                    cos_low, sin_low = cos_v[:8], sin_v[:8]
                    cos_h, cos_l, sin_h, sin_l = [], [], [], []
                    for b in range(0, 8, 2):
                        cos_p, sin_p = [], []
                        for r in (b, b + 1):
                            cos_r = turn_s[pl.ds(at + r, 8, stride=0), :]
                            sin_r = turn_s[pl.ds(at + 8 + r, 8, stride=0), :]
                            cos_p.append(cos_low * cos_r - sin_low * sin_r)
                            sin_p.append(sin_low * cos_r + cos_low * sin_r)
                        high, low = split(jnp.concatenate(cos_p, axis=0))
                        cos_h.append(high)
                        cos_l.append(low)
                        high, low = split(jnp.concatenate(sin_p, axis=0))
                        sin_h.append(high)
                        sin_l.append(low)
                    rights.append(jnp.concatenate(cos_h + sin_h + cos_l + sin_l, axis=0))
                both = dot(lefts[g], jnp.concatenate(rights, axis=1))
                both = both[: 2 * size] + both[2 * size :]
                for k in range(2):
                    u = pair * 2 + k
                    at = (g * 16 + u * 4 + lat_group) * 32
                    real = jnp.zeros((8, 128), f32)
                    imag = jnp.zeros((8, 128), f32)
                    for a in range(SEG_BLOCKS):
                        c = both[a * 8 : a * 8 + 8, k * 128 : (k + 1) * 128]
                        s = both[size + a * 8 : size + a * 8 + 8, k * 128 : (k + 1) * 128]
                        cos_a = turn_s[pl.ds(at + 16 + a, 8, stride=0), :]
                        sin_a = turn_s[pl.ds(at + 24 + a, 8, stride=0), :]
                        real = real + (cos_a * c - sin_a * s)
                        imag = imag - (cos_a * s + sin_a * c)
                    row = u * 32 + g * 16
                    spec_s[row : row + 16, lanes] = jnp.concatenate([real, imag], axis=0)
        turned_s[lanes, :] = spec_s[:, lanes].T
        if lat_group == 0:
            ordering = pltpu.make_async_copy(row_s, order_s, in_sems.at[9])
            leaving = pltpu.make_async_copy(table_s, table_hbm, out_sems.at[0])
            ordering.start()
            leaving.start()
    ordering.wait()
    for place in range(N_LAT):
        span = 32 if place < 8 else 16
        first = place * 32 if place < 8 else 256 + (place - 8) * 16
        start = pl.multiple_of(order_s[0, place] * 32, 32)
        out_s[pl.ds(start, span), :] = turned_s[first : first + span, :]
    sending = pltpu.make_async_copy(out_s, out_hbm, out_sems.at[1])
    sending.start()
    leaving.wait()
    sending.wait()


def recur_kernel(table_ref, row_ref, high_ref, low_ref, poly_s):
    lat_me = lax.axis_index("lat")
    lon_me = lax.axis_index("lon")
    lane = iota((1, 128), 1)
    rows = jnp.zeros((1, 128), jnp.int32)
    for part in range(ROWS_DEV):
        for lat in range(N_LAT):
            rows = jnp.where(lane % 32 == part * 16 + lat, row_ref[lat * 2 + part], rows)
    angle = (NLAT_FULL / 2 - 0.5) - rows.astype(f32)
    _, x = sincos_quarter(jnp.broadcast_to(angle * (math.pi / (4 * NLAT_FULL)), (4, 128)))
    log_sin = 0.5 * jnp.log1p(-x * x)

    table = table_ref[...].astype(bf16)
    found = []
    for q in range(4):
        index = slot_of(q, iota((128, 128), 1) // 32)
        pick = (iota((128, 128), 0) == lon_me * PER_DEV + index) & (index < PER_DEV)
        both = dot(table, pick.astype(f32).astype(bf16))
        mine = jnp.where(iota((N_LAT, 128), 0) == lat_me, both[:N_LAT] + both[N_LAT:], 0.0)
        found.append(jnp.sum(mine, axis=0, keepdims=True))
    number = jnp.concatenate(found, axis=0)
    m = jnp.maximum(number - 1.0, 0.0)
    limit = jnp.where(number > 0.5, MW - m, 0.0)

    z = m + 1.0
    ratio = (z * (z + 1.0) * (z + 2.0) * (z + 3.0)) / (
        (z + 0.5) * (z + 1.5) * (z + 2.5) * (z + 3.5)
    )
    far = 1.0 / (z + 4.0)
    far2 = far * far
    log_ratio = (
        0.5 * jnp.log(z + 4.0)
        + far * (-1.0 / 8 + far2 * (1.0 / 192 - far2 * (1.0 / 640)))
        + jnp.log(ratio)
    )
    log_start = 0.5 * (
        log_ratio - math.lgamma(1.5) + jnp.where(m > 0.5, math.log(2.0), 0.0)
    )
    start = jnp.exp(log_start + m * log_sin)
    twice = 2.0 * m

    unroll = 16

    def turn(t, state):
        previous, current, shrink = state
        base = (t * unroll).astype(f32)
        for j in range(unroll):
            poly_s[pl.ds(pl.multiple_of(t * (unroll * 4), unroll * 4) + j * 4, 4), :] = current
            step = base + (j + 1.0)
            reach = twice + step
            degree2 = reach + step
            square = degree2 * degree2 - 1.0
            gap = step * reach
            root = lax.rsqrt(square * gap)
            grow = square * root
            previous, current = (
                current,
                (grow * x) * current - (grow * shrink) * previous,
            )
            shrink = gap * root
        return previous, current, shrink

    zero = jnp.zeros((4, 128), f32)
    lax.fori_loop(0, MW // unroll, turn, (zero, start, zero))

    for q in range(4):
        for b in range(MW // 128):
            piece = poly_s[pl.ds(b * 512 + q, 128, stride=4), :]
            within = (iota((128, 128), 0) + b * 128).astype(f32) < limit[q : q + 1]
            piece = jnp.where(within, piece, 0.0).T
            high, low = split(piece)
            high_ref[q * 128 : (q + 1) * 128, b * 128 : (b + 1) * 128] = high
            low_ref[q * 128 : (q + 1) * 128, b * 128 : (b + 1) * 128] = low


def back_kernel(in_ref, high_ref, low_ref, out_ref, sum_s, result_s, sems):
    for lat in range(N_LAT):
        total = in_ref[lat * 32 : lat * 32 + 8, :]
        for part in range(1, 4):
            total = total + in_ref[lat * 32 + part * 8 : lat * 32 + part * 8 + 8, :]
        sum_s[lat * 8 : lat * 8 + 8, :] = total
    lane = iota((16, 128), 1)
    lefts = []
    for pair in range(2):
        rows = []
        for half in range(2):
            q = pair * 2 + half
            x = sum_s[pl.ds(q, 16, stride=8), :] + sum_s[pl.ds(q + 4, 16, stride=8), :]
            for u in range(4):
                for part in range(ROWS_DEV):
                    shift = ((half - part) * 16) % 128
                    moved = x if shift == 0 else pltpu.roll(x, shift, 1)
                    at = u * 32 + half * 16
                    rows.append(jnp.where((lane >= at) & (lane < at + 16), moved, 0.0))
        first = jnp.concatenate(rows[:8], axis=0).T
        second = jnp.concatenate(rows[8:], axis=0).T
        lefts.append(split(jnp.concatenate([first, second], axis=1)))
    copies = []
    for b in range(MW // 256):
        lanes = slice(b * 256, (b + 1) * 256)
        for pair in range(2):
            high, low = lefts[pair]
            rows = slice(pair * 256, (pair + 1) * 256)
            both = dot(jnp.concatenate([high, low], axis=0), high_ref[rows, lanes])
            value = both[:128] + both[128:] + dot(high, low_ref[rows, lanes])
            for s in range(8):
                slot = pair * 8 + s
                if slot < PER_DEV:
                    for part in range(2):
                        at = s * 16 + part * 8
                        result_s[slot, :, part, lanes] = value[at : at + 8]
        copy = pltpu.make_async_copy(
            result_s.at[:, :, :, lanes], out_ref.at[:, :, :, lanes], sems.at[b]
        )
        copy.start()
        copies.append(copy)
    for copy in copies:
        copy.wait()


diffusivity = 1.66
scatter_share = 0.2
heat_gain = 10.0


def shards(
    grid_fields, sun_cosine, surface_albedo, gas_absorb, solar_weight, helper_map, row_lat, wave_owner
):
    vmem = pl.BlockSpec(memory_space=pltpu.VMEM)
    smem = pl.BlockSpec(memory_space=pltpu.SMEM)
    hbm = pl.BlockSpec(memory_space=pl.ANY)
    limits = pltpu.CompilerParams(vmem_limit_bytes=16 * 2**20)
    outgoing, table = pl.pallas_call(
        front_kernel,
        out_shape=(
            jax.ShapeDtypeStruct((DESTS * 4, 128), f32),
            jax.ShapeDtypeStruct((2 * N_LAT, 128), f32),
        ),
        in_specs=[hbm] * 8,
        out_specs=(hbm, hbm),
        scratch_shapes=[
            pltpu.VMEM((ROWS_DEV, K, SEG_BLOCKS * BLOCK), f32),
            pltpu.VMEM((ROWS_DEV, SEG_BLOCKS * BLOCK), f32),
            pltpu.VMEM((ROWS_DEV, SEG_BLOCKS * BLOCK), f32),
            pltpu.VMEM((1, G), f32),
            pltpu.VMEM((1, G), f32),
            pltpu.SMEM((ROWS_DEV, SEG_BLOCKS), jnp.int32),
            pltpu.SMEM((ROWS_T,), jnp.int32),
            pltpu.VMEM((MW // 128, 128), jnp.int32),
            pltpu.VMEM((DESTS * 4, 128), f32),
            pltpu.VMEM((8, 128, 128), bf16),
            pltpu.VMEM((G * 8, 128), bf16),
            pltpu.VMEM((128, 128), f32),
            pltpu.VMEM((ROWS_DEV, SEG_BLOCKS * 8, 128), f32),
            pltpu.VMEM((128, 384), f32),
            pltpu.VMEM((1024, 128), f32),
            pltpu.VMEM((16, 128), f32),
            pltpu.VMEM((2 * N_LAT, 128), f32),
            pltpu.VMEM((1, 128), jnp.int32),
            pltpu.SMEM((1, 128), jnp.int32),
            pltpu.VMEM((DESTS * 3, 128), f32),
            pltpu.SemaphoreType.DMA((10,)),
            pltpu.SemaphoreType.DMA((2,)),
        ],
        cost_estimate=pl.CostEstimate(flops=2 * 10**8, bytes_accessed=10**6, transcendentals=10**6),
        name="front",
        compiler_params=pltpu.CompilerParams(vmem_limit_bytes=60 * 2**20),
    )(
        grid_fields,
        sun_cosine,
        surface_albedo,
        gas_absorb.reshape(1, G),
        solar_weight.reshape(1, G),
        helper_map,
        row_lat,
        wave_owner.reshape(MW // 128, 128),
    )
    incoming = lax.all_to_all(
        outgoing.reshape(DESTS, 4, 128), ("lat", "lon"), split_axis=0, concat_axis=0, tiled=True
    )
    high, low = pl.pallas_call(
        recur_kernel,
        out_shape=(
            jax.ShapeDtypeStruct((512, MW), bf16),
            jax.ShapeDtypeStruct((512, MW), bf16),
        ),
        in_specs=[vmem, smem],
        out_specs=(vmem, vmem),
        scratch_shapes=[pltpu.VMEM((MW * 4, 128), f32)],
        cost_estimate=pl.CostEstimate(flops=2 * 10**7, bytes_accessed=3 * 10**6, transcendentals=10**6),
        name="recur",
        compiler_params=limits,
    )(table, row_lat)
    return pl.pallas_call(
        back_kernel,
        out_shape=jax.ShapeDtypeStruct((PER_DEV, K, 2, MW), f32),
        in_specs=[vmem, vmem, vmem],
        out_specs=pl.BlockSpec(memory_space=pl.ANY),
        scratch_shapes=[
            pltpu.VMEM((128, 128), f32),
            pltpu.VMEM((PER_DEV, K, 2, MW), f32),
            pltpu.SemaphoreType.DMA((MW // 256,)),
        ],
        cost_estimate=pl.CostEstimate(flops=5 * 10**8, bytes_accessed=4 * 10**6, transcendentals=0),
        name="back",
        compiler_params=limits,
    )(incoming.reshape(DESTS * 4, 128), high, low)


def solution(mesh):
    placed = (
        P(None, "lat", "lon"),
        P("lat", "lon"),
        P("lat", "lon"),
        P(),
        P(),
        P("lat", "lon"),
        P(),
        P(),
    )
    return jax.shard_map(
        shards,
        mesh=mesh,
        in_specs=placed,
        out_specs=P(("lat", "lon"), None, None, None),
        check_vma=False,
    )
```

```python
import math

import jax
import jax.numpy as jnp
from jax import lax
from jax.experimental import pallas as pl
from jax.experimental.pallas import tpu as pltpu
from jax.sharding import PartitionSpec as P

LEV = 4
BLOCK = 128
NLAT_FULL = 2560
MW = 1280
G = 112
K = 8
SEG_BLOCKS = 6
ROWS_DEV = 2
N_LAT = 16
N_LON = 8
DESTS = N_LAT * N_LON
PER_DEV = 15
MCAP = PER_DEV * N_LON
ROWS_T = N_LAT * ROWS_DEV
LOG2E = math.log2(math.e)

f32 = jnp.float32
bf16 = jnp.bfloat16


def iota(shape, dim):
    return lax.broadcasted_iota(jnp.int32, shape, dim)


def dot(a, b, contract=(1, 0)):
    return lax.dot_general(
        a, b, (((contract[0],), (contract[1],)), ((), ())), preferred_element_type=f32
    )


def split(x):
    high = x.astype(bf16)
    return high, (x - high.astype(f32)).astype(bf16)


def sincos_quarter(r):
    r2 = r * r
    sin_v = r + (r * r2) * (-1.6666654611e-1 + r2 * (8.3321608736e-3 - r2 * 1.9515295891e-4))
    cos_v = 1.0 + r2 * (
        -0.5 + r2 * (4.166664568298827e-2 + r2 * (-1.388731625493765e-3 + r2 * 2.443315711809948e-5))
    )
    for _ in range(2):
        twice = sin_v + sin_v
        cos_v, sin_v = 1.0 - twice * sin_v, twice * cos_v
    return cos_v, sin_v


def slot_of(lane_q, lane_u):
    return (lane_q // 2) * 8 + lane_u * 2 + lane_q % 2


def slot_picks(pick_ref):
    lane = iota((128, 128), 1)
    for u in range(4):
        index = slot_of(lane % 4, u)
        for kind, span in enumerate((N_LON, N_LON // 2)):
            rank = ((lane // 4) % span) * PER_DEV + index
            pick = (iota((128, 128), 0) == rank) & (index < PER_DEV)
            pick_ref[kind * 4 + u] = pick.astype(f32).astype(bf16)


def find_slots(owner_ref, pick_ref, table_ref, order_ref, wave_ref):
    groups = MW // 128
    owner = iota((N_LAT, 128), 0)
    lane = iota((N_LAT, 128), 1)
    hits = [(owner_ref[b : b + 1, :] == owner).astype(f32) for b in range(groups)]
    stacked = jnp.concatenate(hits, axis=0).astype(bf16)
    before = (iota((128, 128), 0) < iota((128, 128), 1)).astype(f32).astype(bf16)
    ahead = dot(stacked, before)
    total = dot(stacked, jnp.ones((128, 128), bf16))
    carry = jnp.zeros((N_LAT, 128), f32)
    table = jnp.zeros((2 * N_LAT, 128), f32)
    for b in range(groups):
        part = slice(b * N_LAT, (b + 1) * N_LAT)
        rank = jnp.sum(hits[b] * (ahead[part] + carry), axis=0, keepdims=True)
        carry = carry + total[part]
        ranked = (rank.astype(jnp.int32) == iota((128, 128), 0)).astype(f32).astype(bf16)
        number = lane + (b * 128 + 1)
        high = ((number >> 4) << 4).astype(f32)
        low = (number & 15).astype(f32)
        both = jnp.concatenate([hits[b] * high, hits[b] * low], axis=0).astype(bf16)
        table = table + dot(both, ranked, (1, 1))
    table_ref[...] = table
    full = carry > (MCAP * 2 / 3)
    below = (iota((N_LAT, N_LAT), 1) < iota((N_LAT, N_LAT), 0)).astype(f32).astype(bf16)
    fulls = dot(below, full.astype(f32).astype(bf16))
    spare = owner.astype(f32) - fulls + N_LAT // 2
    place = jnp.where(full, fulls, spare).astype(jnp.int32)
    order_ref[...] = jnp.sum(jnp.where(place == lane, owner, 0), axis=0, keepdims=True)
    table = table.astype(bf16)
    for u in range(4):
        for kind in range(2):
            found = dot(table, pick_ref[kind * 4 + u])
            found = found[:N_LAT] + found[N_LAT:]
            for g in (0, 1) if kind == 0 else (2,):
                own = place == (g * 4 + lane // 32 if kind == 0 else 8 + lane // 16)
                wave_ref[u * 4 + g : u * 4 + g + 1, :] = jnp.sum(
                    jnp.where(own, found, 0.0), axis=0, keepdims=True
                )


def front_kernel(
    fields_hbm, sun_hbm, ground_hbm, gas_hbm, weight_hbm, lit_hbm, row_hbm, owner_hbm,
    out_hbm, table_hbm,
    fields_ref, sun_ref, ground_ref, gas_ref, weight_ref, lit_ref, row_ref, owner_ref,
    out_s, pick_s, share_s, beam_s, left_s, spec_s, turn_s, wave_ref, table_s, row_s, order_s, turned_s, in_sems, out_sems,
):
    lat_me = lax.axis_index("lat")
    lon_me = lax.axis_index("lon")
    pairs = [
        (owner_hbm, owner_ref),
        (gas_hbm, gas_ref),
        (weight_hbm, weight_ref),
        (row_hbm, row_ref),
        (lit_hbm, lit_ref),
        (sun_hbm, sun_ref),
        (ground_hbm, ground_ref),
    ] + [(fields_hbm.at[:, g, :], fields_ref.at[g]) for g in range(ROWS_DEV)]
    arrivals = [
        pltpu.make_async_copy(source, target, in_sems.at[index])
        for index, (source, target) in enumerate(pairs)
    ]
    for copy in arrivals:
        copy.start()
    slot_picks(pick_s)
    out_s[...] = jnp.zeros_like(out_s)
    arrivals[0].wait()
    for copy in arrivals[1:]:
        copy.wait()
    find_slots(owner_ref, pick_s, table_s, row_s, wave_ref)

    def column(row):
        padded = jnp.concatenate([row, jnp.ones((1, 128 - G), f32)], axis=1)
        return jnp.broadcast_to(padded, (128, 128)).T

    def thirds(x):
        first = x.astype(bf16).astype(f32)
        second = (x - first).astype(bf16).astype(f32)
        return first, second, (x - first - second).astype(bf16).astype(f32)

    kinds = 2 * LEV
    total_weight = jnp.sum(weight_ref[...], axis=1, keepdims=True)
    gas = column(gas_ref[...])
    share = column(weight_ref[...] * (heat_gain / total_weight))
    beam_s[...] = share
    gas_1, gas_2, gas_3 = thirds(gas)
    log_1, log_2, log_3 = thirds(jnp.log2(share))
    lane = iota((8, 128), 1)
    term = lane // kinds
    for part in range(G // 8):
        rows = slice(part * 8, (part + 1) * 8)
        factor = jnp.where(
            (term == 1) | (term == 4), gas_2[rows], jnp.where(term == 2, gas_3[rows], gas_1[rows])
        )
        tail = jnp.where(
            lane < 6 * kinds + 3,
            1.0,
            jnp.where(
                lane == 6 * kinds + 3,
                log_1[rows],
                jnp.where(lane == 6 * kinds + 4, log_2[rows], log_3[rows]),
            ),
        )
        tail = jnp.where((term == 6) & (lane < 6 * kinds + 6), tail, 0.0)
        pieces = []
        for kind in range(kinds):
            own = jnp.where((lane % kinds == kind) & (term < 6), factor, 0.0)
            pieces.append(jnp.where(term == 6, tail, own) if kind < LEV else own)
        share_s[part * 64 : (part + 1) * 64, :] = jnp.concatenate(pieces, axis=0).astype(bf16)

    counts = []
    for g in range(ROWS_DEV):
        row = row_ref[lat_me * ROWS_DEV + g]
        counts.append(20 + 4 * jnp.minimum(row, NLAT_FULL - 1 - row))

    sub = iota((8, BLOCK), 0)
    tile = lambda row: jnp.broadcast_to(row, (8, BLOCK))
    for a in range(SEG_BLOCKS):
        columns = slice(a * BLOCK, (a + 1) * BLOCK)
        paths, grounds, suns = [], [], []
        for g in range(ROWS_DEV):
            x = fields_ref[g, :, columns]
            depth = jnp.maximum(x, 0.0) + jnp.log1p(jnp.exp(-jnp.abs(x)))
            sun = sun_ref[g : g + 1, columns]
            suns.append(sun)
            grounds.append(ground_ref[g : g + 1, columns])
            slant = tile(depth[:1])
            for level in range(1, LEV):
                slant = slant + jnp.where(sub >= level, tile(depth[level : level + 1]), 0.0)
            path = jnp.where(
                sub < LEV,
                slant * (-LOG2E / sun),
                pltpu.roll(depth, LEV, 0) * (-LOG2E * diffusivity),
            )
            path_1, path_2, path_3 = thirds(path)
            logs = thirds(tile(jnp.log2(sun * scatter_share)))
            tail = jnp.where(
                sub == 0, logs[0], jnp.where(sub == 1, logs[1], jnp.where(sub == 2, logs[2], 1.0))
            )
            zero = jnp.zeros((8, BLOCK), f32)
            stack = [path_1, path_1, path_1, path_2, path_2, path_3, tail] + [zero]
            paths.append(jnp.concatenate(stack, axis=0).astype(bf16))
        right = jnp.concatenate(paths, axis=1)
        nets = [[jnp.zeros((8, BLOCK), f32) for _ in range(LEV + 1)] for _ in range(ROWS_DEV)]
        beams = [[jnp.zeros((8, BLOCK), f32) for _ in range(LEV + 1)] for _ in range(ROWS_DEV)]
        for g in range(ROWS_DEV):
            beams[g][0] = tile(suns[g] * (scatter_share * heat_gain / 8))
        ground_b = [tile(ground) for ground in grounds]
        sun_b = [tile(sun * scatter_share) for sun in suns]
        for g in range(ROWS_DEV):
            for part in range(G // 8):
                passing = jnp.exp2(dot(share_s[part * 64 : (part + 1) * 64, :64], paths[g]))
                net, beam_sum = nets[g], beams[g]
                pick = lambda kind: passing[kind * 8 : kind * 8 + 8]
                beam = sun_b[g] * beam_s[part * 8 : (part + 1) * 8, :]
                down, downs, sources = None, [], []
                for level in range(LEV):
                    after = pick(level)
                    source = beam - after
                    beam = after
                    down = source if down is None else down * pick(LEV + level) + source
                    beam_sum[level + 1] = beam_sum[level + 1] + beam
                    downs.append(down)
                    sources.append(source)
                net[LEV] = net[LEV] + down
                upward = ground_b[g] * (beam * (1.0 / scatter_share) + down)
                for level in range(LEV - 1, -1, -1):
                    upward = upward * pick(LEV + level) + sources[level]
                    if level:
                        net[level] = net[level] + (downs[level - 1] - upward)
                    else:
                        net[level] = net[level] - upward
        for g in range(ROWS_DEV):
            levels = [
                net + beam_sum * (1.0 / scatter_share) for net, beam_sum in zip(nets[g], beams[g])
            ]
            levels[LEV] = levels[LEV] * (1.0 - grounds[g])
            is_lit = lit_ref[g, a] >= 0
            heated = fields_ref[g, :, columns]
            for level in range(LEV):
                heat = jnp.sum(levels[level] - levels[level + 1], axis=0, keepdims=True)
                heat = jnp.where(is_lit, heat, 0.0)
                heated = heated + jnp.where(sub == LEV + level, heat, 0.0)
            first = (lon_me * SEG_BLOCKS + a) * BLOCK
            heated = jnp.where(iota((8, BLOCK), 1) + first < counts[g], heated, 0.0)
            left_s[g, a * 8 : (a + 1) * 8, :] = heated

    ordering = pltpu.make_async_copy(row_s, order_s, in_sems.at[9])
    leaving = pltpu.make_async_copy(table_s, table_hbm, out_sems.at[0])
    ordering.start()
    leaving.start()

    offset, place = iota((BLOCK, BLOCK), 0), iota((BLOCK, BLOCK), 1)
    half = BLOCK // 2
    step = place % half
    fold = jnp.where(offset == half + step, 1.0, 0.0)
    mirror = jnp.where(offset == half - 1 - step, 1.0, 0.0)
    fold = (fold + jnp.where(place < half, mirror, -mirror)).astype(bf16)
    size = SEG_BLOCKS * 8
    is_even = iota((size, BLOCK), 1) < half
    lefts = []
    for g in range(ROWS_DEV):
        x = left_s[g]
        first = x.astype(bf16)
        second, third = split(x - first.astype(f32))
        folded = dot(jnp.concatenate([first, second, third], axis=0), fold)
        folded = folded[:size] + (folded[size : 2 * size] + folded[2 * size :])
        evens = split(jnp.where(is_even, folded, 0.0))
        odds = split(jnp.where(is_even, 0.0, folded))
        empty = jnp.zeros((size, BLOCK), bf16)
        lefts.append(
            jnp.concatenate(
                [
                    jnp.concatenate([evens[0], evens[0]], axis=1),
                    jnp.concatenate([odds[0], odds[0]], axis=1),
                    jnp.concatenate([evens[1], empty], axis=1),
                    jnp.concatenate([odds[1], empty], axis=1),
                ],
                axis=0,
            )
        )

    sub = iota((8, 128), 0)
    first_block = (lon_me * SEG_BLOCKS * 2 * BLOCK).astype(f32)
    steps = jnp.concatenate(
        [
            (sub * 2 + 1).astype(f32),
            (sub * 16).astype(f32),
            (sub * (2 * BLOCK) + (BLOCK - 1)).astype(f32) + first_block,
        ],
        axis=0,
    )
    steps = jnp.where(iota((24, 128), 0) < 16 + SEG_BLOCKS, steps, 0.0)
    for lat_group in range(3):
        lanes = slice(lat_group * 128, (lat_group + 1) * 128)
        for pair in range(2):
            for g in range(ROWS_DEV):
                n = jnp.full((1, 128), counts[g] * 2, jnp.int32).astype(f32)
                inverse = 1.0 / n
                scale = lax.rsqrt(n * (ROWS_T / 2))
                rights = []
                for u in (pair * 2, pair * 2 + 1):
                    index = u * 4 + lat_group
                    wave = jnp.maximum(wave_ref[index : index + 1, :] - 1.0, 0.0)
                    phase = steps * wave
                    phase = phase - n * jnp.round(phase * inverse)
                    cos_v, sin_v = sincos_quarter(phase * (inverse * (math.pi / 2)))
                    at = (g * 16 + index) * 32
                    turn_s[at : at + 8, :] = cos_v[8:16]
                    turn_s[at + 8 : at + 16, :] = sin_v[8:16]
                    turn_s[at + 16 : at + 24, :] = cos_v[16:] * scale
                    turn_s[at + 24 : at + 32, :] = sin_v[16:] * scale
                    cos_low, sin_low = cos_v[:8], sin_v[:8]
                    cos_h, cos_l, sin_h, sin_l = [], [], [], []
                    for b in range(0, 8, 2):
                        cos_p, sin_p = [], []
                        for r in (b, b + 1):
                            cos_r = turn_s[pl.ds(at + r, 8, stride=0), :]
                            sin_r = turn_s[pl.ds(at + 8 + r, 8, stride=0), :]
                            cos_p.append(cos_low * cos_r - sin_low * sin_r)
                            sin_p.append(sin_low * cos_r + cos_low * sin_r)
                        high, low = split(jnp.concatenate(cos_p, axis=0))
                        cos_h.append(high)
                        cos_l.append(low)
                        high, low = split(jnp.concatenate(sin_p, axis=0))
                        sin_h.append(high)
                        sin_l.append(low)
                    rights.append(jnp.concatenate(cos_h + sin_h + cos_l + sin_l, axis=0))
                both = dot(lefts[g], jnp.concatenate(rights, axis=1))
                both = both[: 2 * size] + both[2 * size :]
                for k in range(2):
                    u = pair * 2 + k
                    at = (g * 16 + u * 4 + lat_group) * 32
                    real = jnp.zeros((8, 128), f32)
                    imag = jnp.zeros((8, 128), f32)
                    for a in range(SEG_BLOCKS):
                        c = both[a * 8 : a * 8 + 8, k * 128 : (k + 1) * 128]
                        s = both[size + a * 8 : size + a * 8 + 8, k * 128 : (k + 1) * 128]
                        cos_a = turn_s[pl.ds(at + 16 + a, 8, stride=0), :]
                        sin_a = turn_s[pl.ds(at + 24 + a, 8, stride=0), :]
                        real = real + (cos_a * c - sin_a * s)
                        imag = imag - (cos_a * s + sin_a * c)
                    row = u * 32 + g * 16
                    spec_s[row : row + 16, lanes] = jnp.concatenate([real, imag], axis=0)
        turned_s[lanes, :] = spec_s[:, lanes].T
    ordering.wait()
    for place in range(N_LAT):
        span = 32 if place < 8 else 16
        first = place * 32 if place < 8 else 256 + (place - 8) * 16
        start = pl.multiple_of(order_s[0, place] * 32, 32)
        out_s[pl.ds(start, span), :] = turned_s[first : first + span, :]
    sending = pltpu.make_async_copy(out_s, out_hbm, out_sems.at[1])
    sending.start()
    leaving.wait()
    sending.wait()


def recur_kernel(table_ref, row_ref, high_ref, low_ref, poly_s):
    lat_me = lax.axis_index("lat")
    lon_me = lax.axis_index("lon")
    lane = iota((1, 128), 1)
    rows = jnp.zeros((1, 128), jnp.int32)
    for part in range(ROWS_DEV):
        for lat in range(N_LAT):
            rows = jnp.where(lane % 32 == part * 16 + lat, row_ref[lat * 2 + part], rows)
    angle = (NLAT_FULL / 2 - 0.5) - rows.astype(f32)
    _, x = sincos_quarter(jnp.broadcast_to(angle * (math.pi / (4 * NLAT_FULL)), (4, 128)))
    log_sin = 0.5 * jnp.log1p(-x * x)

    table = table_ref[...].astype(bf16)
    found = []
    for q in range(4):
        index = slot_of(q, iota((128, 128), 1) // 32)
        pick = (iota((128, 128), 0) == lon_me * PER_DEV + index) & (index < PER_DEV)
        both = dot(table, pick.astype(f32).astype(bf16))
        mine = jnp.where(iota((N_LAT, 128), 0) == lat_me, both[:N_LAT] + both[N_LAT:], 0.0)
        found.append(jnp.sum(mine, axis=0, keepdims=True))
    number = jnp.concatenate(found, axis=0)
    m = jnp.maximum(number - 1.0, 0.0)
    limit = jnp.where(number > 0.5, MW - m, 0.0)

    z = m + 1.0
    ratio = (z * (z + 1.0) * (z + 2.0) * (z + 3.0)) / (
        (z + 0.5) * (z + 1.5) * (z + 2.5) * (z + 3.5)
    )
    far = 1.0 / (z + 4.0)
    far2 = far * far
    log_ratio = (
        0.5 * jnp.log(z + 4.0)
        + far * (-1.0 / 8 + far2 * (1.0 / 192 - far2 * (1.0 / 640)))
        + jnp.log(ratio)
    )
    log_start = 0.5 * (
        log_ratio - math.lgamma(1.5) + jnp.where(m > 0.5, math.log(2.0), 0.0)
    )
    start = jnp.exp(log_start + m * log_sin)
    twice = 2.0 * m

    unroll = 16

    def turn(t, state):
        previous, current, shrink = state
        base = (t * unroll).astype(f32)
        for j in range(unroll):
            poly_s[pl.ds(pl.multiple_of(t * (unroll * 4), unroll * 4) + j * 4, 4), :] = current
            step = base + (j + 1.0)
            reach = twice + step
            degree2 = reach + step
            square = degree2 * degree2 - 1.0
            gap = step * reach
            root = lax.rsqrt(square * gap)
            grow = square * root
            previous, current = (
                current,
                (grow * x) * current - (grow * shrink) * previous,
            )
            shrink = gap * root
        return previous, current, shrink

    zero = jnp.zeros((4, 128), f32)
    lax.fori_loop(0, MW // unroll, turn, (zero, start, zero))

    for q in range(4):
        for b in range(MW // 128):
            piece = poly_s[pl.ds(b * 512 + q, 128, stride=4), :]
            within = (iota((128, 128), 0) + b * 128).astype(f32) < limit[q : q + 1]
            piece = jnp.where(within, piece, 0.0).T
            high, low = split(piece)
            high_ref[q * 128 : (q + 1) * 128, b * 128 : (b + 1) * 128] = high
            low_ref[q * 128 : (q + 1) * 128, b * 128 : (b + 1) * 128] = low


def back_kernel(in_ref, high_ref, low_ref, out_ref, sum_s, result_s, sems):
    for lat in range(N_LAT):
        total = in_ref[lat * 32 : lat * 32 + 8, :]
        for part in range(1, 4):
            total = total + in_ref[lat * 32 + part * 8 : lat * 32 + part * 8 + 8, :]
        sum_s[lat * 8 : lat * 8 + 8, :] = total
    lane = iota((16, 128), 1)
    lefts = []
    for pair in range(2):
        rows = []
        for half in range(2):
            q = pair * 2 + half
            x = sum_s[pl.ds(q, 16, stride=8), :] + sum_s[pl.ds(q + 4, 16, stride=8), :]
            for u in range(4):
                for part in range(ROWS_DEV):
                    shift = ((half - part) * 16) % 128
                    moved = x if shift == 0 else pltpu.roll(x, shift, 1)
                    at = u * 32 + half * 16
                    rows.append(jnp.where((lane >= at) & (lane < at + 16), moved, 0.0))
        first = jnp.concatenate(rows[:8], axis=0).T
        second = jnp.concatenate(rows[8:], axis=0).T
        lefts.append(split(jnp.concatenate([first, second], axis=1)))
    copies = []
    for b in range(MW // 256):
        lanes = slice(b * 256, (b + 1) * 256)
        for pair in range(2):
            high, low = lefts[pair]
            rows = slice(pair * 256, (pair + 1) * 256)
            both = dot(jnp.concatenate([high, low], axis=0), high_ref[rows, lanes])
            value = both[:128] + both[128:] + dot(high, low_ref[rows, lanes])
            for s in range(8):
                slot = pair * 8 + s
                if slot < PER_DEV:
                    for part in range(2):
                        at = s * 16 + part * 8
                        result_s[slot, :, part, lanes] = value[at : at + 8]
        copy = pltpu.make_async_copy(
            result_s.at[:, :, :, lanes], out_ref.at[:, :, :, lanes], sems.at[b]
        )
        copy.start()
        copies.append(copy)
    for copy in copies:
        copy.wait()


diffusivity = 1.66
scatter_share = 0.2
heat_gain = 10.0


def shards(
    grid_fields, sun_cosine, surface_albedo, gas_absorb, solar_weight, helper_map, row_lat, wave_owner
):
    vmem = pl.BlockSpec(memory_space=pltpu.VMEM)
    smem = pl.BlockSpec(memory_space=pltpu.SMEM)
    hbm = pl.BlockSpec(memory_space=pl.ANY)
    limits = pltpu.CompilerParams(vmem_limit_bytes=16 * 2**20)
    outgoing, table = pl.pallas_call(
        front_kernel,
        out_shape=(
            jax.ShapeDtypeStruct((DESTS * 4, 128), f32),
            jax.ShapeDtypeStruct((2 * N_LAT, 128), f32),
        ),
        in_specs=[hbm] * 8,
        out_specs=(hbm, hbm),
        scratch_shapes=[
            pltpu.VMEM((ROWS_DEV, K, SEG_BLOCKS * BLOCK), f32),
            pltpu.VMEM((ROWS_DEV, SEG_BLOCKS * BLOCK), f32),
            pltpu.VMEM((ROWS_DEV, SEG_BLOCKS * BLOCK), f32),
            pltpu.VMEM((1, G), f32),
            pltpu.VMEM((1, G), f32),
            pltpu.SMEM((ROWS_DEV, SEG_BLOCKS), jnp.int32),
            pltpu.SMEM((ROWS_T,), jnp.int32),
            pltpu.VMEM((MW // 128, 128), jnp.int32),
            pltpu.VMEM((DESTS * 4, 128), f32),
            pltpu.VMEM((8, 128, 128), bf16),
            pltpu.VMEM((G * 8, 128), bf16),
            pltpu.VMEM((128, 128), f32),
            pltpu.VMEM((ROWS_DEV, SEG_BLOCKS * 8, 128), f32),
            pltpu.VMEM((128, 384), f32),
            pltpu.VMEM((1024, 128), f32),
            pltpu.VMEM((16, 128), f32),
            pltpu.VMEM((2 * N_LAT, 128), f32),
            pltpu.VMEM((1, 128), jnp.int32),
            pltpu.SMEM((1, 128), jnp.int32),
            pltpu.VMEM((DESTS * 3, 128), f32),
            pltpu.SemaphoreType.DMA((10,)),
            pltpu.SemaphoreType.DMA((2,)),
        ],
        cost_estimate=pl.CostEstimate(flops=2 * 10**8, bytes_accessed=10**6, transcendentals=10**6),
        name="front",
        compiler_params=pltpu.CompilerParams(vmem_limit_bytes=60 * 2**20),
    )(
        grid_fields,
        sun_cosine,
        surface_albedo,
        gas_absorb.reshape(1, G),
        solar_weight.reshape(1, G),
        helper_map,
        row_lat,
        wave_owner.reshape(MW // 128, 128),
    )
    incoming = lax.all_to_all(
        outgoing.reshape(DESTS, 4, 128), ("lat", "lon"), split_axis=0, concat_axis=0, tiled=True
    )
    high, low = pl.pallas_call(
        recur_kernel,
        out_shape=(
            jax.ShapeDtypeStruct((512, MW), bf16),
            jax.ShapeDtypeStruct((512, MW), bf16),
        ),
        in_specs=[vmem, smem],
        out_specs=(vmem, vmem),
        scratch_shapes=[pltpu.VMEM((MW * 4, 128), f32)],
        cost_estimate=pl.CostEstimate(flops=2 * 10**7, bytes_accessed=3 * 10**6, transcendentals=10**6),
        name="recur",
        compiler_params=limits,
    )(table, row_lat)
    return pl.pallas_call(
        back_kernel,
        out_shape=jax.ShapeDtypeStruct((PER_DEV, K, 2, MW), f32),
        in_specs=[vmem, vmem, vmem],
        out_specs=pl.BlockSpec(memory_space=pl.ANY),
        scratch_shapes=[
            pltpu.VMEM((128, 128), f32),
            pltpu.VMEM((PER_DEV, K, 2, MW), f32),
            pltpu.SemaphoreType.DMA((MW // 256,)),
        ],
        cost_estimate=pl.CostEstimate(flops=5 * 10**8, bytes_accessed=4 * 10**6, transcendentals=0),
        name="back",
        compiler_params=limits,
    )(incoming.reshape(DESTS * 4, 128), high, low)


def solution(mesh):
    placed = (
        P(None, "lat", "lon"),
        P("lat", "lon"),
        P("lat", "lon"),
        P(),
        P(),
        P("lat", "lon"),
        P(),
        P(),
    )
    return jax.shard_map(
        shards,
        mesh=mesh,
        in_specs=placed,
        out_specs=P(("lat", "lon"), None, None, None),
        check_vma=False,
    )
```
